256 devices in a mesh: dp: 32 (over x, z_lo, core), mp: 8 (over y, z_hi).
Axes of the slice: x: 4, y: 4, z: 8 (z_hi: 2, z_lo: 4; z = z_hi * 4 + z_lo), core: 2. Of those that a mesh axis runs over, the one named last changes fastest.
Arguments:
- tokens: bfloat16 [32, 1024, 3584], P('dp'), may hold values from -14 to 14
- modality: int32 [32, 8], P('dp'), may hold values from 0 to 1, as said below
- block_mask: int32 [32, 8, 8], P('dp'), may hold values from 0 to 2, as said below
- q_weight: bfloat16 [2, 3584, 2048], P(None, 'dp', 'mp'), may hold values from -0.09375 to 0.09375
- kv_weight: bfloat16 [2, 3584, 1024], P(None, 'dp'), may hold values from -0.09375 to 0.09375
- o_weight: bfloat16 [2, 2048, 3584], P(None, 'mp', 'dp'), may hold values from -0.125 to 0.125
Outputs:
- attn_out: bfloat16 [32, 1024, 3584], P('dp', 'mp')
The draws below stay inside these ranges and needn't reach their ends.
Inputs may be any that keep to these rules, and one draw needn't show every extreme that they name: modality[s, b] names the section (0 text, 1 image) whose weights serve the 128 tokens of block b of sequence s. block_mask[s, i, j] tells which tokens of block i see block j: 0 none, 1 all, 2 those at or before the query's position; every diagonal entry is 1 or 2, every entry off the diagonal is 0 or 1.
All inputs are finite; a program needn't handle non-finite values.
Results may differ from the reference program's by a relative error of at most 0.015.
Values may be sent and summed in bfloat16 or wider, within the bound.
No kernel may reach another device: no remote copies, remote signals or barrier semaphores. Data moves between devices by JAX's collectives and lax.ppermute only.
A program may use at most 128 MiB of HBM per device.

```python
import jax
import jax.numpy as jnp
from jax import lax

D = 3584
HD = 128
KVH = 4
QHEADS = 16
BLK = 128
SEQ = 1024
SEQS = 32
NBLK = 8
N_MP = 8


def sequence_layout(key):
    subkeys = jax.random.split(key, 4)
    block_place = jnp.arange(NBLK, dtype=jnp.int32)
    doc_rate = jax.random.randint(subkeys[0], (), 1, NBLK + 1)
    doc_start = (jax.random.randint(subkeys[1], (NBLK,), 0, 4 * NBLK) < doc_rate) | (block_place == 0)
    run_start = doc_start | (jax.random.randint(subkeys[2], (NBLK,), 0, 3) == 0)
    doc_id = jnp.cumsum(doc_start.astype(jnp.int32)) - 1
    run_id = jnp.cumsum(run_start.astype(jnp.int32)) - 1
    run_kind = jax.random.randint(subkeys[3], (NBLK,), 0, 2)
    block_kinds = run_kind[run_id].astype(jnp.int32)
    row_index = block_place[:, None]
    col_index = block_place[None, :]
    same_doc = doc_id[:, None] == doc_id[None, :]
    lower_ok = (col_index < row_index) & same_doc
    upper_ok = (col_index > row_index) & (run_id[:, None] == run_id[None, :]) & (block_kinds[:, None] == 1)
    diag_value = jnp.where(block_kinds == 1, 1, 2).astype(jnp.int32)
    mask_table = jnp.where(row_index == col_index, diag_value[:, None], jnp.where(lower_ok | upper_ok, 1, 0))
    return (block_kinds, mask_table.astype(jnp.int32))


def all_layouts(key):
    return jax.vmap(sequence_layout)(jax.random.split(jax.random.fold_in(key, 17), SEQS))


def draw_modality(key, part):
    return all_layouts(key)[0]


def draw_block_mask(key, part):
    return all_layouts(key)[1]


def draw_tokens(key, part):
    drawn = jnp.clip(jax.random.normal(key, (SEQS, SEQ, D), jnp.float32), -6.0, 6.0)
    return drawn.astype(jnp.bfloat16)


def block_scale(key, dims, cuts, smallest, top_value):
    factor_of = 1.0
    for dim, parts in cuts:
        heights = jax.random.uniform(jax.random.fold_in(jax.random.fold_in(key, 6), dim), (parts,), jnp.float32, smallest / len(cuts), top_value / len(cuts))
        factor_of = factor_of * jnp.repeat(jnp.exp(heights), dims[dim] // parts).reshape((-1,) + (1,) * (len(dims) - 1 - dim))
    return factor_of


def noise(stream_key, extent, scale, limit, shards=(), kind=jnp.bfloat16):
    values = scale * jax.random.normal(stream_key, extent, jnp.float32)
    if shards:
        values = values * block_scale(stream_key, extent, shards, -0.22, 0.18)
    return jnp.clip(values, -limit, limit).astype(kind)


def setup_inputs(seed: int = 0) -> dict:
    key_list = jax.random.split(jax.random.key(seed), 7)
    return {
        "tokens": draw_tokens(jax.random.fold_in(key_list[6], 71), 0),
        "modality": draw_modality(jax.random.fold_in(key_list[6], 71), 0),
        "block_mask": draw_block_mask(jax.random.fold_in(key_list[6], 71), 0),
        "q_weight": noise(key_list[3], (2, D, QHEADS * HD), D ** -0.5, 0.09375, ((1, 32), (2, 8))),
        "kv_weight": noise(key_list[4], (2, D, 2 * KVH * HD), D ** -0.5, 0.09375, ((1, 32),)),
        "o_weight": noise(key_list[5], (2, QHEADS * HD, D), (QHEADS * HD) ** -0.5, 0.125, ((1, 8), (2, 32))),
    }


rope_theta = 1000000.0


def rotary_tables(length, head_width):
    half_width = head_width // 2
    frequency = rope_theta ** (-jnp.arange(half_width, dtype=jnp.float32) * 2.0 / head_width)
    angles = jnp.arange(length, dtype=jnp.float32)[:, None] * frequency[None, :]
    angles = jnp.concatenate([angles, angles], axis=1)
    return jnp.cos(angles), jnp.sin(angles)


def rotate(values, cosine_table, sine_table):
    half_width = values.shape[-1] // 2
    turned = jnp.concatenate([-values[..., half_width:], values[..., :half_width]], axis=-1)
    return values * cosine_table[:, None, :] + turned * sine_table[:, None, :]


def allowed_pairs(layout, first_row, block_rows, length):
    block_count = length // BLK
    rows_mask = lax.dynamic_slice_in_dim(layout, first_row // BLK, block_rows // BLK, 0)
    expanded = jnp.broadcast_to(rows_mask[:, None, :, None], (block_rows // BLK, BLK, block_count, BLK)).reshape(block_rows, length)
    positions = jnp.arange(length, dtype=jnp.int32)
    query_pos = first_row + jnp.arange(block_rows, dtype=jnp.int32)
    return (expanded == 1) | ((expanded == 2) & (positions[None, :] <= query_pos[:, None]))


def reference(tokens, modality, block_mask, q_weight, kv_weight, o_weight):
    group_size = QHEADS // KVH
    block_rows = min(512, SEQ)
    cosine_table, sine_table = rotary_tables(SEQ, HD)
    score_scale = HD ** -0.5
    group_cols = QHEADS * HD // N_MP

    def one_sequence(inputs):
        states, block_kinds, layout = inputs
        blocks = states.reshape(NBLK, BLK, D)

        def project(pieces):
            row_block, block_kind = pieces
            query_weight = lax.dynamic_index_in_dim(q_weight, block_kind, 0, keepdims=False)
            pair_weight = lax.dynamic_index_in_dim(kv_weight, block_kind, 0, keepdims=False)
            return (jnp.dot(row_block, query_weight, preferred_element_type=jnp.float32),
                    jnp.dot(row_block, pair_weight, preferred_element_type=jnp.float32))

        query_raw, pair_raw = lax.map(project, (blocks, block_kinds))
        queries = rotate(query_raw.reshape(SEQ, QHEADS, HD), cosine_table, sine_table)
        queries = queries.astype(jnp.bfloat16).reshape(SEQ, KVH, group_size, HD)
        pairs = pair_raw.reshape(SEQ, KVH, 2, HD)
        key_heads = rotate(pairs[:, :, 0], cosine_table, sine_table).astype(jnp.bfloat16)
        value_heads = pairs[:, :, 1].astype(jnp.bfloat16)

        def attend(block_index):
            first_row = block_index * block_rows
            query_part = lax.dynamic_slice_in_dim(queries, first_row, block_rows, 0)
            allowed = allowed_pairs(layout, first_row, block_rows, SEQ)
            scores = jnp.einsum("qgjd,kgd->gjqk", query_part.astype(jnp.float32), key_heads.astype(jnp.float32)) * score_scale
            scores = jnp.where(allowed[None, None], scores, -1e30)
            row_max = jnp.max(scores, axis=-1, keepdims=True)
            weights = jnp.exp(scores - row_max)
            weights = (weights / jnp.sum(weights, axis=-1, keepdims=True)).astype(jnp.bfloat16)
            mixed_out = jnp.einsum("gjqk,kgd->qgjd", weights.astype(jnp.float32), value_heads.astype(jnp.float32))
            return mixed_out.astype(jnp.bfloat16).reshape(block_rows, QHEADS * HD)

        attended = lax.map(attend, jnp.arange(SEQ // block_rows, dtype=jnp.int32))
        attended = attended.reshape(NBLK, BLK, N_MP, group_cols)

        def finish(pieces):
            row_block, block_kind = pieces
            out_weight = lax.dynamic_index_in_dim(o_weight, block_kind, 0, keepdims=False).reshape(N_MP, group_cols, D)
            group_parts = jnp.einsum("kgc,gcd->gkd", row_block.astype(jnp.float32), out_weight.astype(jnp.float32))
            group_parts = lax.optimization_barrier(group_parts.astype(jnp.bfloat16)).astype(jnp.float32)
            return jnp.sum(group_parts, axis=0).astype(jnp.bfloat16)

        return lax.map(finish, (attended, block_kinds)).reshape(SEQ, D)

    return lax.map(one_sequence, (tokens, modality, block_mask))
```

```python
import functools

import jax
import jax.numpy as jnp
import numpy as np
from jax import lax
from jax.experimental import pallas as pl
from jax.experimental.pallas import tpu as pltpu
from jax.sharding import Mesh
from jax.sharding import PartitionSpec as P

D = 3584
HD = 128
BLK = 128
NBLK = 8
SEQ = 1024
ROWS = 112
NG = 32
NY = 4
QB = 4
HEADS = 4
WID = HEADS * HD
ROPE_THETA = 1000000.0
NEG = -1e30
ANY = pl.BlockSpec(memory_space=pl.ANY)
SM = pl.BlockSpec(memory_space=pltpu.SMEM)


def rotary_tables():
    half = HD // 2
    freq = ROPE_THETA ** (-np.arange(half, dtype=np.float64) * 2.0 / HD)
    ang = np.arange(SEQ, dtype=np.float64)[:, None] * freq[None, :]
    cos = np.concatenate([np.cos(ang), np.cos(ang)], axis=1)
    sin = np.concatenate([-np.sin(ang), np.sin(ang)], axis=1)
    return np.asarray(cos, np.float32), np.asarray(sin, np.float32)


def rotate(x, cos, sin):
    return x * cos + pltpu.roll(x, HD // 2, 1) * sin


def kv_body(mod, x_hbm, w_hbm, cos, sin, k_out, v_out, x, w, xsem, wsem):
    copies = []
    for m in range(2):
        c = pltpu.make_async_copy(w_hbm.at[:, m], w.at[m], wsem.at[m])
        c.start()
        copies.append(c)
    xc = []
    for b in range(NBLK):
        c = pltpu.make_async_copy(x_hbm.at[pl.ds(b * BLK, BLK)], x.at[b], xsem.at[b])
        c.start()
        xc.append(c)
    for c in copies:
        c.wait()
    for b in range(NBLK):
        xc[b].wait()
        y = jnp.dot(x[b], w[mod[b]].reshape(D, 2 * HD), preferred_element_type=jnp.float32)
        rows = pl.ds(b * BLK, BLK)
        k_out[rows, :] = rotate(y[:, :HD], cos[rows, :], sin[rows, :]).astype(jnp.bfloat16)
        v_out[rows, :] = y[:, HD:].astype(jnp.bfloat16)


def q_body(mod, pos, mask, x_hbm, w_hbm, cos, sin, k, v, att, x, w, q, s, xsem, wsem):
    zh = pos[1]
    copies = []
    for h in range(2):
        for g in range(4):
            for m in range(2):
                c = pltpu.make_async_copy(
                    w_hbm.at[g, h, :, m],
                    w.at[m, pl.ds(8 * g, 8), :, pl.ds(h * 2 * HD, 2 * HD)],
                    wsem.at[m],
                )
                c.start()
                copies.append(c)
    xc = []
    for i in range(QB):
        c = pltpu.make_async_copy(
            x_hbm.at[pl.ds((2 * i + zh) * BLK, BLK)], x.at[i], xsem.at[i]
        )
        c.start()
        xc.append(c)
    for c in copies:
        c.wait()
    for c in xc:
        c.wait()
    diff = lax.broadcasted_iota(jnp.int32, (BLK, BLK), 1) - lax.broadcasted_iota(
        jnp.int32, (BLK, BLK), 0
    )
    diff = jnp.concatenate([diff] * HEADS, axis=0)

    def one(i, carry):
        b = 2 * i + zh
        y = jnp.dot(x[i], w[mod[b]].reshape(D, WID), preferred_element_type=jnp.float32)
        rows = pl.ds(pl.multiple_of(b * BLK, BLK), BLK)
        ct, st = cos[rows, :], sin[rows, :]
        for h in range(HEADS):
            q[h * BLK : (h + 1) * BLK, :] = rotate(y[:, h * HD : (h + 1) * HD], ct, st).astype(
                jnp.bfloat16
            )
        qq = q[...]
        for j in range(NBLK):
            mb = mask[b, j]
            off = jnp.where(mb == 1, 4096, jnp.where(mb == 2, BLK * (b - j), -4096))
            sj = lax.dot_general(
                qq,
                k[j * BLK : (j + 1) * BLK, :],
                (((1,), (1,)), ((), ())),
                preferred_element_type=jnp.float32,
            )
            s[:, j * BLK : (j + 1) * BLK] = jnp.where(diff <= off, sj, NEG)
        sv = s[...]
        p = jnp.exp((sv - jnp.max(sv, axis=1, keepdims=True)) * (HD**-0.5))
        total = jnp.sum(p, axis=1, keepdims=True)
        a = jnp.dot(p.astype(jnp.bfloat16), v[...], preferred_element_type=jnp.float32) / total
        for h in range(HEADS):
            att[i, :, h * HD : (h + 1) * HD] = a[h * BLK : (h + 1) * BLK, :].astype(jnp.bfloat16)
        return carry

    lax.fori_loop(0, QB, one, 0)


def o_body(mod, pos, att, w_hbm, o0, o1, o2, o3, w, wsem):
    y0, zh = pos[0], pos[1]
    copies = []
    for h in range(2):
        for g in range(4):
            for m in range(2):
                c = pltpu.make_async_copy(
                    w_hbm.at[g, h, :, 2 + m],
                    w.at[m, pl.ds(8 * g, 8), :, pl.ds(h * 2 * HD, 2 * HD)],
                    wsem.at[m],
                )
                c.start()
                copies.append(c)
    for c in copies:
        c.wait()
    for s, out in ((2, o2), (1, o1), (3, o3), (0, o0)):
        i = lax.rem(y0 + s, NY)
        wm = w.at[mod[2 * i + zh]]
        a = att[i]
        for g in range(4):
            wt = wm[8 * g : 8 * g + 8].reshape(8 * ROWS, WID)
            r = lax.dot_general(a, wt, (((1,), (1,)), ((), ())), preferred_element_type=jnp.float32)
            out[:, g * 8 * ROWS : (g + 1) * 8 * ROWS] = r.astype(jnp.bfloat16)


VM = pl.BlockSpec(memory_space=pltpu.VMEM)
BF = jnp.bfloat16


def kv_call(mod, x, w, cos, sin):
    return pl.pallas_call(
        kv_body,
        out_shape=[jax.ShapeDtypeStruct((SEQ, HD), BF)] * 2,
        in_specs=[SM, ANY, ANY, VM, VM],
        out_specs=[VM, VM],
        scratch_shapes=[
            pltpu.VMEM((NBLK, BLK, D), BF),
            pltpu.VMEM((2, NG, ROWS, 2 * HD), BF),
            pltpu.SemaphoreType.DMA((NBLK,)),
            pltpu.SemaphoreType.DMA((2,)),
        ],
        cost_estimate=pl.CostEstimate(
            flops=2 * SEQ * D * 2 * HD, bytes_accessed=2 * SEQ * D + 8 * D * HD, transcendentals=0
        ),
    )(mod, x, w, cos, sin)


def q_call(mod, pos, mask, x, w, cos, sin, k, v):
    return pl.pallas_call(
        q_body,
        out_shape=jax.ShapeDtypeStruct((QB, BLK, WID), BF),
        in_specs=[SM, SM, SM, ANY, ANY, VM, VM, VM, VM],
        out_specs=VM,
        scratch_shapes=[
            pltpu.VMEM((QB, BLK, D), BF),
            pltpu.VMEM((2, NG, ROWS, WID), BF),
            pltpu.VMEM((HEADS * BLK, HD), BF),
            pltpu.VMEM((HEADS * BLK, SEQ), jnp.float32),
            pltpu.SemaphoreType.DMA((QB,)),
            pltpu.SemaphoreType.DMA((2,)),
        ],
        cost_estimate=pl.CostEstimate(
            flops=2 * QB * BLK * D * WID + 4 * QB * BLK * SEQ * WID,
            bytes_accessed=SEQ * D + 4 * D * WID,
            transcendentals=QB * BLK * HEADS * SEQ,
        ),
    )(mod, pos, mask, x, w, cos, sin, k, v)


def o_call(mod, pos, att, w):
    return pl.pallas_call(
        o_body,
        out_shape=[jax.ShapeDtypeStruct((BLK, D), BF)] * 4,
        in_specs=[SM, SM, VM, ANY],
        out_specs=[VM] * 4,
        scratch_shapes=[
            pltpu.VMEM((2, NG, ROWS, WID), BF),
            pltpu.SemaphoreType.DMA((2,)),
        ],
        cost_estimate=pl.CostEstimate(
            flops=2 * QB * BLK * D * WID, bytes_accessed=4 * D * WID, transcendentals=0
        ),
    )(mod, pos, att, w)


def local(tokens, modality, block_mask, q_weight, kv_weight, o_weight):
    y = lax.axis_index("y")
    zh = lax.axis_index("zh")
    pos = jnp.stack([y, zh]).astype(jnp.int32)
    mod = modality[0]
    mask = block_mask[0]
    x = tokens[0]
    cos, sin = (jnp.asarray(t) for t in rotary_tables())
    kv = lax.dynamic_slice_in_dim(kv_weight, y * (2 * HD), 2 * HD, 2)
    qo = jnp.concatenate([q_weight, jnp.swapaxes(o_weight, 1, 2)], axis=0)
    kv_all = lax.all_gather(kv, ("x", "zl", "c"), axis=0)
    qo_all = lax.all_gather(qo, ("x", "zh", "zl", "c"), axis=0)
    qo_all = qo_all.reshape(4, 2, 8, 4, ROWS, 2 * HD)
    k, v = kv_call(mod, x, kv_all, cos, sin)
    att = q_call(mod, pos, mask, x, qo_all, cos, sin, k, v)
    outs = o_call(mod, pos, att, qo_all)
    total = outs[0].astype(jnp.float32)
    for s in (2, 1, 3):
        got = lax.ppermute(outs[s], "y", [(i, (i + s) % NY) for i in range(NY)])
        total = total + got.astype(jnp.float32)
    return total.astype(BF)[None]


def solution(mesh):
    fine = Mesh(mesh.devices.reshape(4, 4, 2, 4, 2), ("x", "zl", "c", "y", "zh"))
    dp = ("x", "zl", "c")
    mp = ("y", "zh")
    in_specs = (
        P(dp, None, None),
        P(dp, None),
        P(dp, None, None),
        P(None, dp, mp),
        P(None, dp, None),
        P(None, mp, dp),
    )
    return jax.shard_map(
        local, mesh=fine, in_specs=in_specs, out_specs=P(dp, mp, None), check_vma=False
    )
```

```python
import functools

import jax
import jax.numpy as jnp
import numpy as np
from jax import lax
from jax.experimental import pallas as pl
from jax.experimental.pallas import tpu as pltpu
from jax.sharding import Mesh
from jax.sharding import PartitionSpec as P

D = 3584
HD = 128
BLK = 128
NBLK = 8
SEQ = 1024
ROWS = 112
NG = 32
NY = 4
QB = 4
HEADS = 4
WID = HEADS * HD
ROPE_THETA = 1000000.0
NEG = -1e30
ANY = pl.BlockSpec(memory_space=pl.ANY)
SM = pl.BlockSpec(memory_space=pltpu.SMEM)


def rotary_tables():
    half = HD // 2
    freq = ROPE_THETA ** (-np.arange(half, dtype=np.float64) * 2.0 / HD)
    ang = np.arange(SEQ, dtype=np.float64)[:, None] * freq[None, :]
    cos = np.concatenate([np.cos(ang), np.cos(ang)], axis=1)
    sin = np.concatenate([-np.sin(ang), np.sin(ang)], axis=1)
    return np.asarray(cos, np.float32), np.asarray(sin, np.float32)


def rotate(x, cos, sin):
    return x * cos + pltpu.roll(x, HD // 2, 1) * sin


def place(lin, partner):
    zh = lin & 1
    c = (lin >> 3) & 1
    zl = (lin >> 4) & 3
    x = (lin >> 6) & 3
    return x, zh * 4 + zl, (1 - c if partner else c)


FIRST, SECOND = (0, -1, 1, -2), (2, -3, 3, 4)
DX = (0, -1, 1, 2)
DZ_OF = (0, -1, 1, -2, 2, -3, 3, 4)
X_OF = ((0, FIRST), (-1, FIRST), (1, FIRST), (-1, SECOND), (1, SECOND), (2, FIRST), (2, SECOND), (0, SECOND))


def piece(lin, partner, a, j):
    x, z, cc = place(lin, partner)
    dx = jnp.where(cc == 0, DX[j], X_OF[a][0])
    dz = jnp.where(cc == 0, DZ_OF[a], X_OF[a][1][j])
    xs, zs = (x + dx) & 3, (z + dz) & 7
    return (xs * 4 + (zs & 3)) * 2 + cc, zs >> 2


def kv_piece(lin, partner, a, j):
    x, z, cc = place(lin, partner)
    dx = jnp.where(cc == 0, DX[j], DX[a])
    dz = jnp.where(cc == 0, DX[a], DX[j])
    return (((x + dx) & 3) * 4 + ((z + dz) & 3)) * 2 + cc


def fetch(lin, refs, w, sem):
    copies = []
    for n, ref in enumerate(refs):
        for j in range(4):
            g, zh = piece(lin, n >= 8, n % 8, j)
            cols = pl.ds(pl.multiple_of(zh * (2 * HD), 2 * HD), 2 * HD)
            c = pltpu.make_async_copy(ref.at[j], w.at[:, g, :, cols], sem)
            c.start()
            copies.append(c)
    return copies


def kv_body(mod, pos, *refs):
    pieces, (x_hbm, cos, sin, k_out, v_out, x, w, xsem, wsem) = refs[:10], refs[10:]
    lin = pos[0]
    copies = []
    for n in range(2):
        b, t1p, t1m, t2p, t2m = pieces[5 * n : 5 * n + 5]
        for a, ref in enumerate((b, t1p, t1m, None)):
            for j in range(4):
                g = kv_piece(lin, n == 1, a, j)
                for m in range(2):
                    s = ref.at[m, j] if ref is not None else (t2p, t2m)[m].at[j]
                    c = pltpu.make_async_copy(s, w.at[m, g], wsem)
                    c.start()
                    copies.append(c)
    xc = []
    for b in range(NBLK):
        c = pltpu.make_async_copy(x_hbm.at[pl.ds(b * BLK, BLK)], x.at[b], xsem.at[b])
        c.start()
        xc.append(c)
    for c in copies:
        c.wait()
    for b in range(NBLK):
        xc[b].wait()
        y = jnp.dot(x[b], w[mod[b]].reshape(D, 2 * HD), preferred_element_type=jnp.float32)
        rows = pl.ds(b * BLK, BLK)
        k_out[rows, :] = rotate(y[:, :HD], cos[rows, :], sin[rows, :]).astype(jnp.bfloat16)
        v_out[rows, :] = y[:, HD:].astype(jnp.bfloat16)


def q_body(mod, pos, mask, *refs):
    x_hbm, cos, sin, k, v, att, x, w, q, s, xsem, wsem = refs[16:]
    zh = pos[0] & 1
    copies = fetch(pos[0], refs[:16], w, wsem)
    xc = []
    for i in range(QB):
        c = pltpu.make_async_copy(
            x_hbm.at[pl.ds((2 * i + zh) * BLK, BLK)], x.at[i], xsem.at[i]
        )
        c.start()
        xc.append(c)
    for c in copies:
        c.wait()
    for c in xc:
        c.wait()
    diff = lax.broadcasted_iota(jnp.int32, (BLK, BLK), 1) - lax.broadcasted_iota(
        jnp.int32, (BLK, BLK), 0
    )
    diff = jnp.concatenate([diff] * HEADS, axis=0)

    def one(i, carry):
        b = 2 * i + zh
        y = jnp.dot(x[i], w[mod[b]].reshape(D, WID), preferred_element_type=jnp.float32)
        rows = pl.ds(pl.multiple_of(b * BLK, BLK), BLK)
        ct, st = cos[rows, :], sin[rows, :]
        for h in range(HEADS):
            q[h * BLK : (h + 1) * BLK, :] = rotate(y[:, h * HD : (h + 1) * HD], ct, st).astype(
                jnp.bfloat16
            )
        qq = q[...]
        for j in range(NBLK):
            mb = mask[b, j]
            off = jnp.where(mb == 1, 4096, jnp.where(mb == 2, BLK * (b - j), -4096))
            sj = lax.dot_general(
                qq,
                k[j * BLK : (j + 1) * BLK, :],
                (((1,), (1,)), ((), ())),
                preferred_element_type=jnp.float32,
            )
            s[:, j * BLK : (j + 1) * BLK] = jnp.where(diff <= off, sj, NEG)
        sv = s[...]
        p = jnp.exp((sv - jnp.max(sv, axis=1, keepdims=True)) * (HD**-0.5))
        total = jnp.sum(p, axis=1, keepdims=True)
        a = jnp.dot(p.astype(jnp.bfloat16), v[...], preferred_element_type=jnp.float32) / total
        for h in range(HEADS):
            att[i, :, h * HD : (h + 1) * HD] = a[h * BLK : (h + 1) * BLK, :].astype(jnp.bfloat16)
        return carry

    lax.fori_loop(0, QB, one, 0)


def o_body(mod, pos, *refs):
    att, o0, o1, o2, o3, w, wsem = refs[16:]
    y0, zh = (pos[0] >> 1) & 3, pos[0] & 1
    copies = fetch(pos[0], refs[:16], w, wsem)
    for c in copies:
        c.wait()
    for s, out in ((2, o2), (1, o1), (3, o3), (0, o0)):
        i = lax.rem(y0 + s, NY)
        wm = w.at[mod[2 * i + zh]]
        a = att[i]
        for g in range(4):
            wt = wm[8 * g : 8 * g + 8].reshape(8 * ROWS, WID)
            r = lax.dot_general(a, wt, (((1,), (1,)), ((), ())), preferred_element_type=jnp.float32)
            out[:, g * 8 * ROWS : (g + 1) * 8 * ROWS] = r.astype(jnp.bfloat16)


VM = pl.BlockSpec(memory_space=pltpu.VMEM)
BF = jnp.bfloat16


def kv_call(mod, pos, pieces, x, cos, sin):
    return pl.pallas_call(
        kv_body,
        out_shape=[jax.ShapeDtypeStruct((SEQ, HD), BF)] * 2,
        in_specs=[SM, SM] + [ANY] * 11 + [VM, VM],
        out_specs=[VM, VM],
        scratch_shapes=[
            pltpu.VMEM((NBLK, BLK, D), BF),
            pltpu.VMEM((2, NG, ROWS, 2 * HD), BF),
            pltpu.SemaphoreType.DMA((NBLK,)),
            pltpu.SemaphoreType.DMA,
        ],
        name="kvproj",
        cost_estimate=pl.CostEstimate(
            flops=2 * SEQ * D * 2 * HD, bytes_accessed=2 * SEQ * D + 8 * D * HD, transcendentals=0
        ),
    )(mod, pos, *pieces, x, cos, sin)


def q_call(mod, pos, mask, pieces, x, cos, sin, k, v):
    return pl.pallas_call(
        q_body,
        out_shape=jax.ShapeDtypeStruct((QB, BLK, WID), BF),
        in_specs=[SM, SM, SM] + [ANY] * 17 + [VM, VM, VM, VM],
        out_specs=VM,
        scratch_shapes=[
            pltpu.VMEM((QB, BLK, D), BF),
            pltpu.VMEM((2, NG, ROWS, WID), BF),
            pltpu.VMEM((HEADS * BLK, HD), BF),
            pltpu.VMEM((HEADS * BLK, SEQ), jnp.float32),
            pltpu.SemaphoreType.DMA((QB,)),
            pltpu.SemaphoreType.DMA,
        ],
        name="qattend",
        cost_estimate=pl.CostEstimate(
            flops=2 * QB * BLK * D * WID + 4 * QB * BLK * SEQ * WID,
            bytes_accessed=SEQ * D + 4 * D * WID,
            transcendentals=QB * BLK * HEADS * SEQ,
        ),
    )(mod, pos, mask, *pieces, x, cos, sin, k, v)


def o_call(mod, pos, pieces, att):
    return pl.pallas_call(
        o_body,
        out_shape=[jax.ShapeDtypeStruct((BLK, D), BF)] * 4,
        in_specs=[SM, SM] + [ANY] * 16 + [VM],
        out_specs=[VM] * 4,
        scratch_shapes=[
            pltpu.VMEM((2, NG, ROWS, WID), BF),
            pltpu.SemaphoreType.DMA,
        ],
        name="oproj",
        cost_estimate=pl.CostEstimate(
            flops=2 * QB * BLK * D * WID, bytes_accessed=4 * D * WID, transcendentals=0
        ),
    )(mod, pos, *pieces, att)


AXES = ("x", "zl", "c", "zh")


def pairs(step, x_core, only=None):
    out = []
    for x in range(4):
        for z in range(8):
            for c in range(2):
                if only is not None and c != only:
                    continue
                tx, tz = ((x + step) % 4, z) if c == x_core else (x, (z + step) % 8)
                out.append(
                    tuple(((i * 4 + (k & 3)) * 2 + c) * 2 + (k >> 2) for i, k in ((x, z), (tx, tz)))
                )
    return out


def send(a, step, x_core, only=None):
    return lax.ppermute(a, AXES, pairs(step, x_core, only))


def swap(a):
    return lax.ppermute(a, "c", [(0, 1), (1, 0)])


def spread(kv, q, o, c):
    own = jnp.concatenate([kv[:1], q, o, kv[1:]], axis=0)
    r1p, r1m = send(own, 1, 0), send(own, -1, 0)
    r2p, r2m = send(r1p[:5], 1, 0), send(r1m[1:], -1, 0)
    kv_own = jnp.stack(
        [
            jnp.stack([own[0], r1p[0], r1m[0], r2p[0]]),
            jnp.stack([own[5], r1p[5], r1m[5], r2m[4]]),
        ]
    )
    k1p, k1m = send(kv_own, 1, 1), send(kv_own, -1, 1)
    k2p, k2m = send(k1p[0], 1, 1), send(k1m[1], -1, 1)
    kv_own = [kv_own, k1p, k1m, k2p, k2m]
    kv_all = kv_own + [swap(t) for t in kv_own]
    r3p, r3m = send(r2p[1:], 1, 0, 1), send(r2m[:4], -1, 0, 1)
    r4p, r4m = send(r3p[:2], 1, 0, 1), send(r3m[2:], -1, 0, 1)
    res = []
    for k, last in ((0, r4p), (2, r4m)):
        b = jnp.stack([own[1 + k : 3 + k], r1p[1 + k : 3 + k], r1m[1 + k : 3 + k], r2p[1 + k : 3 + k]])
        b2 = jnp.stack([r2m[k : k + 2], r3p[k : k + 2], r3m[k : k + 2], last])
        t1p, t1m = send(b, 1, 1), send(b, -1, 1)
        t2p = send(jnp.where(c == 0, t1p, b2), 1, 1)
        t2m = send(jnp.where(c == 0, t1m, b2), -1, 1)
        t3p = send(jnp.where(c == 0, t2p, t1p), 1, 1)
        t3m = send(t2m, -1, 1)
        t4p, t4m = send(t3p[:2], 1, 1, 0), send(t3m[2:], -1, 1, 0)
        u = jnp.where(c == 0, jnp.concatenate([t4p, t4m]), b2)
        mine = [b, t1p, t1m, t2p, t2m, t3p, t3m, u]
        res.append(mine + [swap(t) for t in mine])
    return kv_all, res[0], res[1]


def local(tokens, modality, block_mask, q_weight, kv_weight, o_weight):
    y = lax.axis_index("y")
    c = lax.axis_index("c")
    pos = lax.axis_index(("x", "zl", "c", "y", "zh")).astype(jnp.int32).reshape(1)
    mod = modality[0]
    mask = block_mask[0]
    x = tokens[0]
    cos, sin = (jnp.asarray(t) for t in rotary_tables())
    kv = lax.dynamic_slice_in_dim(kv_weight, y * (2 * HD), 2 * HD, 2)
    kv_all, q_all, o_all = spread(kv, q_weight, jnp.swapaxes(o_weight, 1, 2), c)
    k, v = kv_call(mod, pos, kv_all, x, cos, sin)
    att = q_call(mod, pos, mask, q_all, x, cos, sin, k, v)
    o0, o1, o2, o3 = o_call(mod, pos, o_all, att)
    up = [(i, (i + 1) % NY) for i in range(NY)]
    down = [(i, (i - 1) % NY) for i in range(NY)]
    half = D // 2
    f32 = jnp.float32
    a = lax.ppermute(o2[:, :half], "y", up)
    b = lax.ppermute(o2[:, half:], "y", down)
    p = jnp.concatenate([(o1[:, :half].astype(f32) + a.astype(f32)).astype(BF), o1[:, half:]], 1)
    m = jnp.concatenate([o3[:, :half], (o3[:, half:].astype(f32) + b.astype(f32)).astype(BF)], 1)
    p = lax.ppermute(p, "y", up)
    m = lax.ppermute(m, "y", down)
    return (o0.astype(f32) + p.astype(f32) + m.astype(f32)).astype(BF)[None]


def solution(mesh):
    fine = Mesh(mesh.devices.reshape(4, 4, 2, 4, 2), ("x", "zl", "c", "y", "zh"))
    dp = ("x", "zl", "c")
    mp = ("y", "zh")
    in_specs = (
        P(dp, None, None),
        P(dp, None),
        P(dp, None, None),
        P(None, dp, mp),
        P(None, dp, None),
        P(None, mp, dp),
    )
    return jax.shard_map(
        local, mesh=fine, in_specs=in_specs, out_specs=P(dp, mp, None), check_vma=False
    )
```

```python
import functools

import jax
import jax.numpy as jnp
import numpy as np
from jax import lax
from jax.experimental import pallas as pl
from jax.experimental.pallas import tpu as pltpu
from jax.sharding import Mesh
from jax.sharding import PartitionSpec as P

D = 3584
HD = 128
BLK = 128
NBLK = 8
SEQ = 1024
ROWS = 112
NG = 32
NY = 4
QB = 4
HEADS = 4
WID = HEADS * HD
ROPE_THETA = 1000000.0
NEG = -1e30
ANY = pl.BlockSpec(memory_space=pl.ANY)
SM = pl.BlockSpec(memory_space=pltpu.SMEM)


def rotary_tables():
    half = HD // 2
    freq = ROPE_THETA ** (-np.arange(half, dtype=np.float64) * 2.0 / HD)
    freq = np.concatenate([freq, freq])[None, :]
    fine = np.arange(BLK, dtype=np.float64)[:, None] * freq
    base = BLK * np.arange(NBLK, dtype=np.float64)[:, None] * freq
    return [np.asarray(t, np.float32) for t in (np.cos(fine), np.sin(fine), np.cos(base), np.sin(base))]


def block_tables(tables, b):
    cf, sf = tables[0][...], tables[1][...]
    cb, sb = tables[2][pl.ds(b, 1), :], tables[3][pl.ds(b, 1), :]
    sign = jnp.where(lax.broadcasted_iota(jnp.int32, (1, HD), 1) < HD // 2, -1.0, 1.0)
    return cb * cf - sb * sf, sign * (sb * cf + cb * sf)


def rotate(x, cos, sin):
    return x * cos + pltpu.roll(x, HD // 2, 1) * sin


def assign(kinds, inv):
    n = len(kinds)
    n1 = sum(kinds)
    h0 = (n - n1 + 1) // 2
    for s in range(n + 2):
        inv[s] = -1
    c0, c1, slots = 0, 0, []
    for b, kind in enumerate(kinds):
        slot = jnp.where(kind == 0, c0, 2 * h0 + c1)
        inv[slot] = b
        slots.append(slot)
        c0, c1 = c0 + 1 - kind, c1 + kind
    return slots, h0, h0 + (n1 + 1) // 2


def place(lin, partner):
    zh = lin & 1
    c = (lin >> 3) & 1
    zl = (lin >> 4) & 3
    x = (lin >> 6) & 3
    return x, zh * 4 + zl, (1 - c if partner else c)


FIRST, SECOND = (0, -1, 1, -2), (2, -3, 3, 4)
DX = (0, -1, 1, 2)
DZ_OF = (0, -1, 1, -2, 2, -3, 3, 4)
X_OF = ((0, FIRST), (-1, FIRST), (1, FIRST), (-1, SECOND), (1, SECOND), (2, FIRST), (2, SECOND), (0, SECOND))


def piece(lin, partner, a, j):
    x, z, cc = place(lin, partner)
    dx = jnp.where(cc == 0, DX[j], X_OF[a][0])
    dz = jnp.where(cc == 0, DZ_OF[a], X_OF[a][1][j])
    xs, zs = (x + dx) & 3, (z + dz) & 7
    return (xs * 4 + (zs & 3)) * 2 + cc, zs >> 2


def kv_piece(lin, partner, a, j):
    x, z, cc = place(lin, partner)
    dx = jnp.where(cc == 0, DX[j], DX[a])
    dz = jnp.where(cc == 0, DX[a], DX[j])
    return (((x + dx) & 3) * 4 + ((z + dz) & 3)) * 2 + cc


def fetch(lin, refs, w, sem):
    copies = []
    for n in range(16):
        for j in range(4):
            if n < 8:
                src = refs[n].at[j]
            else:
                k = (0, 0, 0, 1, 1, 2, 2, 3)[n - 8]
                src = refs[8 + k].at[4 * (n - 8 - (0, 3, 5, 7)[k]) + j]
            g, zh = piece(lin, n >= 8, n % 8, j)
            cols = pl.ds(pl.multiple_of(zh * (2 * HD), 2 * HD), 2 * HD)
            c = pltpu.make_async_copy(src, w.at[:, g, :, cols], sem)
            c.start()
            copies.append(c)
    return copies


def kv_body(mod, pos, *refs):
    pieces, tables, (k_out, v_out, x, w, inv, xsem, wsem) = refs[:7], refs[8:12], refs[12:]
    x_hbm = refs[7]
    lin = pos[0]
    slots, h0, passes = assign([mod[b] for b in range(NBLK)], inv)
    copies = []
    for b in range(NBLK):
        c = pltpu.make_async_copy(x_hbm.at[pl.ds(b * BLK, BLK)], x.at[slots[b]], xsem.at[b])
        c.start()
        copies.append(c)
    for n in range(2):
        for a in range(4):
            for j in range(4):
                g = kv_piece(lin, n == 1, a, j)
                for m in range(2):
                    if n == 0:
                        src = pieces[a].at[m, j] if a < 3 else pieces[3 + m].at[j]
                    else:
                        src = pieces[5].at[2 * a + m, j] if a < 3 else pieces[6].at[m, j]
                    c = pltpu.make_async_copy(src, w.at[m, g], wsem)
                    c.start()
                    copies.append(c)
    for c in copies:
        c.wait()

    def one(p, carry):
        sec = jnp.where(p >= h0, 1, 0)
        lhs = x[pl.ds(2 * p, 2)].reshape(2 * BLK, D)
        y = jnp.dot(lhs, w[sec].reshape(D, 2 * HD), preferred_element_type=jnp.float32)
        for t in range(2):
            b = inv[2 * p + t]

            @pl.when(b >= 0)
            def _():
                yt = y[t * BLK : (t + 1) * BLK]
                cos, sin = block_tables(tables, b)
                rows = pl.ds(pl.multiple_of(b * BLK, BLK), BLK)
                k_out[rows, :] = rotate(yt[:, :HD], cos, sin).astype(jnp.bfloat16)
                v_out[rows, :] = yt[:, HD:].astype(jnp.bfloat16)

        return carry

    lax.fori_loop(0, passes, one, 0)


def q_body(mod, pos, mask, *refs):
    x_hbm, tables, (k, v, att, x, w, q, s, inv, xsem, wsem) = refs[12], refs[13:17], refs[17:]
    zh = pos[0] & 1
    slots, h0, passes = assign([mod[2 * i + zh] for i in range(QB)], inv)
    copies = []
    for i in range(QB):
        c = pltpu.make_async_copy(
            x_hbm.at[pl.ds((2 * i + zh) * BLK, BLK)], x.at[slots[i]], xsem.at[i]
        )
        c.start()
        copies.append(c)
    copies += fetch(pos[0], refs[:12], w, wsem)
    for c in copies:
        c.wait()

    def project(p, carry):
        sec = jnp.where(p >= h0, 1, 0)
        lhs = x[pl.ds(2 * p, 2)].reshape(2 * BLK, D)
        y = jnp.dot(lhs, w[sec].reshape(D, WID), preferred_element_type=jnp.float32)
        for t in range(2):
            i = inv[2 * p + t]

            @pl.when(i >= 0)
            def _():
                cos, sin = block_tables(tables, 2 * i + zh)
                for h in range(HEADS):
                    yt = y[t * BLK : (t + 1) * BLK, h * HD : (h + 1) * HD]
                    q[i, h * BLK : (h + 1) * BLK, :] = rotate(yt, cos, sin).astype(jnp.bfloat16)

        return carry

    lax.fori_loop(0, passes, project, 0)
    diff = lax.broadcasted_iota(jnp.int32, (BLK, BLK), 1) - lax.broadcasted_iota(
        jnp.int32, (BLK, BLK), 0
    )
    diff = jnp.concatenate([diff] * HEADS, axis=0)

    def one(i, carry):
        b = 2 * i + zh
        qq = q[i]
        for j in range(NBLK):
            mb = mask[b, j]
            off = jnp.where(mb == 1, 4096, jnp.where(mb == 2, BLK * (b - j), -4096))
            sj = lax.dot_general(
                qq,
                k[j * BLK : (j + 1) * BLK, :],
                (((1,), (1,)), ((), ())),
                preferred_element_type=jnp.float32,
            )
            s[:, j * BLK : (j + 1) * BLK] = jnp.where(diff <= off, sj, NEG)
        sv = s[...]
        p = jnp.exp((sv - jnp.max(sv, axis=1, keepdims=True)) * (HD**-0.5))
        total = jnp.sum(p, axis=1, keepdims=True)
        a = jnp.dot(p.astype(jnp.bfloat16), v[...], preferred_element_type=jnp.float32) / total
        for h in range(HEADS):
            att[i, :, h * HD : (h + 1) * HD] = a[h * BLK : (h + 1) * BLK, :].astype(jnp.bfloat16)
        return carry

    lax.fori_loop(0, QB, one, 0)


def o_body(mod, pos, *refs):
    att, outs, (w, a, inv, wsem) = refs[12], refs[13:21], refs[21:]
    y0, zh = (pos[0] >> 1) & 3, pos[0] & 1
    copies = fetch(pos[0], refs[:12], w, wsem)
    slots, h0, passes = assign([mod[2 * i + zh] for i in range(QB)], inv)
    for i in range(QB):
        a[slots[i]] = att[i]
    for c in copies:
        c.wait()
    quarter = D // 4

    def one(p, carry):
        sec = jnp.where(p >= h0, 1, 0)
        lhs = a[pl.ds(2 * p, 2)].reshape(2 * BLK, WID)
        place_of = [jnp.where(inv[2 * p + t] < 0, -1, (inv[2 * p + t] - y0) & 3) for t in range(2)]
        for g in range(4):
            wt = w[sec, 8 * g : 8 * g + 8].reshape(quarter, WID)
            r = lax.dot_general(
                lhs, wt, (((1,), (1,)), ((), ())), preferred_element_type=jnp.float32
            ).astype(jnp.bfloat16)
            cols = slice((g % 2) * quarter, (g % 2 + 1) * quarter)
            for t in range(2):
                for n in range(4):

                    @pl.when(place_of[t] == n)
                    def _():
                        outs[2 * n + g // 2][:, cols] = r[t * BLK : (t + 1) * BLK]

        return carry

    lax.fori_loop(0, passes, one, 0)


VM = pl.BlockSpec(memory_space=pltpu.VMEM)
BF = jnp.bfloat16


def kv_call(mod, pos, pieces, x, tables):
    return pl.pallas_call(
        kv_body,
        out_shape=[jax.ShapeDtypeStruct((SEQ, HD), BF)] * 2,
        in_specs=[SM, SM] + [ANY] * 8 + [VM] * 4,
        out_specs=[VM, VM],
        scratch_shapes=[
            pltpu.VMEM((NBLK + 2, BLK, D), BF),
            pltpu.VMEM((2, NG, ROWS, 2 * HD), BF),
            pltpu.SMEM((NBLK + 2,), jnp.int32),
            pltpu.SemaphoreType.DMA((NBLK,)),
            pltpu.SemaphoreType.DMA,
        ],
        name="kvproj",
        cost_estimate=pl.CostEstimate(
            flops=2 * SEQ * D * 2 * HD, bytes_accessed=2 * SEQ * D + 8 * D * HD, transcendentals=0
        ),
    )(mod, pos, *pieces, x, *tables)


def q_call(mod, pos, mask, pieces, x, tables, k, v):
    return pl.pallas_call(
        q_body,
        out_shape=jax.ShapeDtypeStruct((QB, BLK, WID), BF),
        in_specs=[SM, SM, SM] + [ANY] * 13 + [VM] * 6,
        out_specs=VM,
        scratch_shapes=[
            pltpu.VMEM((QB + 2, BLK, D), BF),
            pltpu.VMEM((2, NG, ROWS, WID), BF),
            pltpu.VMEM((QB, HEADS * BLK, HD), BF),
            pltpu.VMEM((HEADS * BLK, SEQ), jnp.float32),
            pltpu.SMEM((QB + 2,), jnp.int32),
            pltpu.SemaphoreType.DMA((QB,)),
            pltpu.SemaphoreType.DMA,
        ],
        name="qattend",
        cost_estimate=pl.CostEstimate(
            flops=2 * QB * BLK * D * WID + 4 * QB * BLK * SEQ * WID,
            bytes_accessed=SEQ * D + 4 * D * WID,
            transcendentals=QB * BLK * HEADS * SEQ,
        ),
    )(mod, pos, mask, *pieces, x, *tables, k, v)


def o_call(mod, pos, pieces, att):
    return pl.pallas_call(
        o_body,
        out_shape=[jax.ShapeDtypeStruct((BLK, D // 2), BF)] * 8,
        in_specs=[SM, SM] + [ANY] * 12 + [VM],
        out_specs=[VM] * 8,
        scratch_shapes=[
            pltpu.VMEM((2, NG, ROWS, WID), BF),
            pltpu.VMEM((QB + 2, BLK, WID), BF),
            pltpu.SMEM((QB + 2,), jnp.int32),
            pltpu.SemaphoreType.DMA,
        ],
        name="oproj",
        cost_estimate=pl.CostEstimate(
            flops=2 * QB * BLK * D * WID, bytes_accessed=4 * D * WID, transcendentals=0
        ),
    )(mod, pos, *pieces, att)


AXES = ("x", "zl", "c", "zh")


def pairs(step, x_core, only=None):
    out = []
    for x in range(4):
        for z in range(8):
            for c in range(2):
                if only is not None and c != only:
                    continue
                tx, tz = ((x + step) % 4, z) if c == x_core else (x, (z + step) % 8)
                out.append(
                    tuple(((i * 4 + (k & 3)) * 2 + c) * 2 + (k >> 2) for i, k in ((x, z), (tx, tz)))
                )
    return out


def send(a, step, x_core, only=None):
    return lax.ppermute(a, AXES, pairs(step, x_core, only))


def swap(a):
    return lax.ppermute(a, "c", [(0, 1), (1, 0)])


def after(a, *deps):
    return lax.optimization_barrier((a, *deps))[0]


def gather_start(kv, q, o):
    own = jnp.concatenate([kv[:1], q, o, kv[1:]], axis=0)
    r1p, r1m = send(own, 1, 0), send(own, -1, 0)
    r2p, r2m = send(r1p[:5], 1, 0), send(r1m[1:], -1, 0)
    return own, r1p, r1m, r2p, r2m


def gather_kv(own, r1p, r1m, r2p, r2m):
    b = jnp.stack(
        [
            jnp.stack([own[0], r1p[0], r1m[0], r2p[0]]),
            jnp.stack([own[5], r1p[5], r1m[5], r2m[4]]),
        ]
    )
    t1p, t1m = send(b, 1, 1), send(b, -1, 1)
    t2p, t2m = send(t1p[0], 1, 1), send(t1m[1], -1, 1)
    return [b, t1p, t1m, t2p, t2m, swap(jnp.concatenate([b, t1p, t1m])), swap(jnp.stack([t2p, t2m]))]


def bundles(first, r3p, r3m, last, k):
    own, r1p, r1m, r2p, r2m = first
    b = jnp.stack([t[1 + k : 3 + k] for t in (own, r1p, r1m, r2p)])
    return b, jnp.stack([r2m[k : k + 2], r3p[k : k + 2], r3m[k : k + 2], last])


def local(tokens, modality, block_mask, q_weight, kv_weight, o_weight):
    y = lax.axis_index("y")
    c = lax.axis_index("c")
    pos = lax.axis_index(("x", "zl", "c", "y", "zh")).astype(jnp.int32).reshape(1)
    mod = modality[0]
    mask = block_mask[0]
    x = tokens[0]
    tables = [jnp.asarray(t) for t in rotary_tables()]
    kv = lax.dynamic_slice_in_dim(kv_weight, y * (2 * HD), 2 * HD, 2)
    first = gather_start(kv, q_weight, jnp.swapaxes(o_weight, 1, 2))
    kv_all = gather_kv(*first)
    r2p, r2m = first[3:]
    r3p, r3m = send(r2p[1:], 1, 0, 1), send(r2m[:4], -1, 0, 1)
    r4p, r4m = send(r3p[:2], 1, 0, 1), send(r3m[2:], -1, 0, 1)
    qb, qb2 = bundles(first, r3p, r3m, r4p, 0)
    ob, ob2 = bundles(first, r3p, r3m, r4m, 2)
    mine = c == 0
    q1p, q1m = send(qb, 1, 1), send(qb, -1, 1)
    q2p, q2m = send(jnp.where(mine, q1p, qb2), 1, 1), send(jnp.where(mine, q1m, qb2), -1, 1)
    ob = after(ob, q1p, q1m)
    o1p, o1m = send(ob, 1, 1), send(ob, -1, 1)
    q3p, q3m = send(jnp.where(mine, q2p, q1p), 1, 1), send(q2m, -1, 1)
    k, v = kv_call(mod, pos, kv_all, x, tables)
    o2p, o2m = send(jnp.where(mine, o1p, ob2), 1, 1), send(jnp.where(mine, o1m, ob2), -1, 1)
    q4p, q4m = send(q3p[:2], 1, 1, 0), send(q3m[2:], -1, 1, 0)
    qu = jnp.where(mine, jnp.concatenate([q4p, q4m]), qb2)
    q_all = [qb, q1p, q1m, q2p, q2m, q3p, q3m, qu]
    q_all += [swap(jnp.concatenate(t)) for t in ((qb, q1p, q1m), (q2p, q2m), (q3p, q3m), (qu,))]
    o3p = send(after(jnp.where(mine, o2p, o1p), k), 1, 1)
    o3m = send(after(o2m, k), -1, 1)
    att = q_call(mod, pos, mask, q_all, x, tables, k, v)
    o4p = send(after(o3p[:2], att), 1, 1, 0)
    o4m = send(after(o3m[2:], att), -1, 1, 0)
    ou = jnp.where(mine, jnp.concatenate([o4p, o4m]), ob2)
    o_all = [ob, o1p, o1m, o2p, o2m, o3p, o3m, ou]
    o_all += [swap(jnp.concatenate(t)) for t in ((ob, o1p, o1m), (o2p, o2m), (o3p, o3m), (ou,))]
    o0a, o0b, o1a, o1b, o2a, o2b, o3a, o3b = o_call(mod, pos, o_all, att)
    up = [(i, (i + 1) % NY) for i in range(NY)]
    down = [(i, (i - 1) % NY) for i in range(NY)]
    f32 = jnp.float32

    def add(a, b):
        return (a.astype(f32) + b.astype(f32)).astype(BF)

    far_a, far_b = lax.ppermute(o2a, "y", up), lax.ppermute(o2b, "y", down)
    pb, ma = lax.ppermute(o1b, "y", up), lax.ppermute(o3a, "y", down)
    pa = lax.ppermute(add(o1a, far_a), "y", up)
    mb = lax.ppermute(add(o3b, far_b), "y", down)
    out_a = (o0a.astype(f32) + pa.astype(f32) + ma.astype(f32)).astype(BF)
    out_b = (o0b.astype(f32) + pb.astype(f32) + mb.astype(f32)).astype(BF)
    return jnp.concatenate([out_a, out_b], axis=1)[None]


def solution(mesh):
    fine = Mesh(mesh.devices.reshape(4, 4, 2, 4, 2), ("x", "zl", "c", "y", "zh"))
    dp = ("x", "zl", "c")
    mp = ("y", "zh")
    in_specs = (
        P(dp, None, None),
        P(dp, None),
        P(dp, None, None),
        P(None, dp, mp),
        P(None, dp, None),
        P(None, mp, dp),
    )
    return jax.shard_map(
        local, mesh=fine, in_specs=in_specs, out_specs=P(dp, mp, None), check_vma=False
    )
```

```python
import functools

import jax
import jax.numpy as jnp
import numpy as np
from jax import lax
from jax.experimental import pallas as pl
from jax.experimental.pallas import tpu as pltpu
from jax.sharding import Mesh
from jax.sharding import PartitionSpec as P

D = 3584
HD = 128
BLK = 128
NBLK = 8
SEQ = 1024
ROWS = 112
NG = 32
NY = 4
QB = 4
HEADS = 4
WID = HEADS * HD
ROPE_THETA = 1000000.0
NEG = -1e30
ANY = pl.BlockSpec(memory_space=pl.ANY)
SM = pl.BlockSpec(memory_space=pltpu.SMEM)


def rotary_tables():
    half = HD // 2
    freq = ROPE_THETA ** (-np.arange(half, dtype=np.float64) * 2.0 / HD)
    freq = np.concatenate([freq, freq])[None, :]
    fine = np.arange(BLK, dtype=np.float64)[:, None] * freq
    base = BLK * np.arange(NBLK, dtype=np.float64)[:, None] * freq
    return [np.asarray(t, np.float32) for t in (np.cos(fine), np.sin(fine), np.cos(base), np.sin(base))]


def block_tables(tables, b):
    cf, sf = tables[0][...], tables[1][...]
    cb, sb = tables[2][pl.ds(b, 1), :], tables[3][pl.ds(b, 1), :]
    sign = jnp.where(lax.broadcasted_iota(jnp.int32, (1, HD), 1) < HD // 2, -1.0, 1.0)
    return cb * cf - sb * sf, sign * (sb * cf + cb * sf)


def rotate(x, cos, sin):
    return x * cos + pltpu.roll(x, HD // 2, 1) * sin


FIRST, SECOND = (0, -1, 1, -2), (2, -3, 3, 4)
DX = (0, -1, 1, 2)
DZ_OF = (0, -1, 1, -2, 2, -3, 3, 4)
X_OF = ((0, FIRST), (-1, FIRST), (1, FIRST), (-1, SECOND), (1, SECOND), (2, FIRST), (2, SECOND), (0, SECOND))


def piece_tables(x, z, c):
    cc = jnp.stack([c, 1 - c])[:, None, None]
    dx = jnp.where(cc == 0, np.array(DX)[None, None, :], np.array([t[0] for t in X_OF])[None, :, None])
    dz = jnp.where(cc == 0, np.array(DZ_OF)[None, :, None], np.array([t[1] for t in X_OF])[None])
    xs, zs = (x + dx) & 3, (z + dz) & 7
    wide = ((xs * 4 + (zs & 3)) * 2 + cc) * 2 + (zs >> 2)
    d = np.array(DX)
    dx = jnp.where(cc == 0, d[None, None, :], d[None, :, None])
    dz = jnp.where(cc == 0, d[None, :, None], d[None, None, :])
    narrow = (((x + dx) & 3) * 4 + ((z + dz) & 3)) * 2 + cc
    return jnp.concatenate([wide.reshape(64), narrow.reshape(32)]).astype(jnp.int32)


def fetch(tab, refs, w, sem):
    base = 0
    for ref in refs:

        def start(j, carry, ref=ref, base=base):
            at = tab[base + j]
            cols = pl.ds(pl.multiple_of((at & 1) * (2 * HD), 2 * HD), 2 * HD)
            pltpu.make_async_copy(ref.at[j], w.at[:, at >> 1, :, cols], sem).start()
            return carry

        lax.fori_loop(0, ref.shape[0], start, 0)
        base += ref.shape[0]


def attend(i, zh, mask, q, k, v, s):
    b = 2 * i + zh
    diff = lax.broadcasted_iota(jnp.int32, (BLK, BLK), 1) - lax.broadcasted_iota(
        jnp.int32, (BLK, BLK), 0
    )
    diff = jnp.concatenate([diff] * HEADS, axis=0)
    qq = q[i]
    for j in range(NBLK):
        mb = mask[b, j]
        off = jnp.where(mb == 1, 4096, jnp.where(mb == 2, BLK * (b - j), -4096))
        sj = lax.dot_general(
            qq,
            k[j * BLK : (j + 1) * BLK, :],
            (((1,), (1,)), ((), ())),
            preferred_element_type=jnp.float32,
        )
        s[:, j * BLK : (j + 1) * BLK] = jnp.where(diff <= off, sj, NEG)
    sv = s[...]
    p = jnp.exp((sv - jnp.max(sv, axis=1, keepdims=True)) * (HD**-0.5))
    total = jnp.sum(p, axis=1, keepdims=True)
    a = jnp.dot(p.astype(BF), v[...], preferred_element_type=jnp.float32) / total
    a = a.astype(BF)
    return jnp.concatenate([a[h * BLK : (h + 1) * BLK] for h in range(HEADS)], axis=1)


def project_out(a, w, sec, outs):
    quarter = D // 4
    for g in range(4):
        wt = w[sec, 8 * g : 8 * g + 8].reshape(quarter, WID)
        r = lax.dot_general(a, wt, (((1,), (1,)), ((), ())), preferred_element_type=jnp.float32)
        outs[g // 2][:, (g % 2) * quarter : (g % 2 + 1) * quarter] = r.astype(BF)


def head_body(mod, pos, mask, tab, *refs):
    kv_refs, q_refs, o_refs, x_hbm, tables = refs[:7], refs[7:19], refs[19:31], refs[31], refs[32:36]
    q, k, v = refs[36:39]
    outs = refs[39:41]
    x, wk, wq, wo, s, inv, xsem, ksem, qsem, osem = refs[41:]
    y0, zh = pos[0], pos[1]
    for a in range(4):

        def start(j, carry, a=a):
            at = [tab[64 + n * 16 + a * 4 + j] for n in range(2)]
            if a < 3:
                pltpu.make_async_copy(kv_refs[a].at[:, j], wk.at[:, at[0]], ksem).start()
                src = kv_refs[5].at[pl.ds(2 * a, 2), j]
            else:
                for m in range(2):
                    pltpu.make_async_copy(kv_refs[3 + m].at[j], wk.at[m, at[0]], ksem).start()
                src = kv_refs[6].at[:, j]
            pltpu.make_async_copy(src, wk.at[:, at[1]], ksem).start()
            return carry

        lax.fori_loop(0, 4, start, 0)
    order = [2 * i + zh for i in range(QB)] + [2 * i + 1 - zh for i in range(QB)]
    kinds = [mod[b] for b in order]
    n1 = sum(kinds)
    h0 = (NBLK - n1 + 1) // 2
    passes = h0 + (n1 + 1) // 2
    for t in range(NBLK + 2):
        inv[t] = -1
    c0, c1 = 0, 0
    for n, (b, kind) in enumerate(zip(order, kinds)):
        inv[jnp.where(kind == 0, c0, 2 * h0 + c1)] = b
        c0, c1 = c0 + 1 - kind, c1 + kind
        if n == QB - 1:
            p0, p1 = (c0 + 1) // 2, (c1 + 1) // 2

    def block_copy(t):
        rows = pl.ds(pl.multiple_of(inv[t] * BLK, BLK), BLK)
        return pltpu.make_async_copy(x_hbm.at[rows], x.at[t], xsem.at[t])

    def start_x(t, carry):
        @pl.when(inv[t] >= 0)
        def _():
            block_copy(t).start()

        return carry

    lax.fori_loop(0, NBLK + 2, start_x, 0)
    fetch(tab, q_refs, wq, qsem)
    fetch(tab, o_refs, wo, osem)
    pltpu.make_async_copy(wk, wk, ksem).wait()

    def project_kv(p, carry):
        sec = jnp.where(p >= h0, 1, 0)
        ids = [inv[2 * p + t] for t in range(2)]
        for t in range(2):

            @pl.when(ids[t] >= 0)
            def _():
                block_copy(2 * p + t).wait()

        lhs = x[pl.ds(2 * p, 2)].reshape(2 * BLK, D)
        y = jnp.dot(lhs, wk[sec].reshape(D, 2 * HD), preferred_element_type=jnp.float32)
        for t in range(2):

            @pl.when(ids[t] >= 0)
            def _():
                yt = y[t * BLK : (t + 1) * BLK]
                cos, sin = block_tables(tables, ids[t])
                rows = pl.ds(pl.multiple_of(ids[t] * BLK, BLK), BLK)
                k[rows, :] = rotate(yt[:, :HD], cos, sin).astype(BF)
                v[rows, :] = yt[:, HD:].astype(BF)

        return carry

    lax.fori_loop(0, passes, project_kv, 0)
    pltpu.make_async_copy(wq, wq, qsem).wait()

    def project_q(p, carry):
        sec = jnp.where(p >= p0, 1, 0)
        slot = jnp.where(p >= p0, 2 * (h0 + p - p0), 2 * p)
        lhs = x[pl.ds(slot, 2)].reshape(2 * BLK, D)
        y = jnp.dot(lhs, wq[sec].reshape(D, WID), preferred_element_type=jnp.float32)
        for t in range(2):
            b = inv[slot + t]

            @pl.when((b >= 0) & ((b & 1) == zh))
            def _():
                cos, sin = block_tables(tables, b)
                for h in range(HEADS):
                    yt = y[t * BLK : (t + 1) * BLK, h * HD : (h + 1) * HD]
                    q[b >> 1, h * BLK : (h + 1) * BLK, :] = rotate(yt, cos, sin).astype(BF)

        return carry

    lax.fori_loop(0, p0 + p1, project_q, 0)
    far = (y0 + 2) & 3
    a = attend(far, zh, mask, q, k, v, s)
    pltpu.make_async_copy(wo, wo, osem).wait()
    project_out(a, wo, mod[2 * far + zh], outs)


def tail_body(rels, mod, pos, mask, tab, *refs):
    o_refs, (q, k, v), outs, (wo, att, s, osem) = refs[:12], refs[12:15], refs[15:-4], refs[-4:]
    y0, zh = pos[0], pos[1]
    fetch(tab, o_refs, wo, osem)

    def one(n, carry):
        att[n] = attend((y0 + rels[0] + 2 * n) & 3, zh, mask, q, k, v, s)
        return carry

    lax.fori_loop(0, len(rels), one, 0)
    pltpu.make_async_copy(wo, wo, osem).wait()
    for n, rel in enumerate(rels):
        project_out(att[n], wo, mod[2 * ((y0 + rel) & 3) + zh], outs[2 * n : 2 * n + 2])


VM = pl.BlockSpec(memory_space=pltpu.VMEM)
BF = jnp.bfloat16
HALF_BLOCK = jax.ShapeDtypeStruct((BLK, D // 2), BF)


def head(mod, pos, mask, tab, kv_all, q_all, o_all, x, tables):
    return pl.pallas_call(
        head_body,
        out_shape=[
            jax.ShapeDtypeStruct((QB, HEADS * BLK, HD), BF),
            jax.ShapeDtypeStruct((SEQ, HD), BF),
            jax.ShapeDtypeStruct((SEQ, HD), BF),
            HALF_BLOCK,
            HALF_BLOCK,
        ],
        in_specs=[SM] * 4 + [ANY] * 32 + [VM] * 4,
        out_specs=[VM] * 5,
        scratch_shapes=[
            pltpu.VMEM((NBLK + 2, BLK, D), BF),
            pltpu.VMEM((2, NG, ROWS, 2 * HD), BF),
            pltpu.VMEM((2, NG, ROWS, WID), BF),
            pltpu.VMEM((2, NG, ROWS, WID), BF),
            pltpu.VMEM((HEADS * BLK, SEQ), jnp.float32),
            pltpu.SMEM((NBLK + 2,), jnp.int32),
            pltpu.SemaphoreType.DMA((NBLK + 2,)),
            pltpu.SemaphoreType.DMA,
            pltpu.SemaphoreType.DMA,
            pltpu.SemaphoreType.DMA,
        ],
        compiler_params=pltpu.CompilerParams(vmem_limit_bytes=44 << 20),
        name="head",
        cost_estimate=pl.CostEstimate(
            flops=2 * SEQ * D * 2 * HD + 2 * QB * BLK * D * WID,
            bytes_accessed=2 * SEQ * D + 8 * D * HD + 8 * D * WID,
            transcendentals=BLK * HEADS * SEQ,
        ),
    )(mod, pos, mask, tab, *kv_all, *q_all, *o_all, x, *tables)


def tail(rels, mod, pos, mask, tab, o_all, q, k, v):
    n = len(rels)
    return pl.pallas_call(
        functools.partial(tail_body, rels),
        out_shape=[HALF_BLOCK] * (2 * n),
        in_specs=[SM] * 4 + [ANY] * 12 + [VM] * 3,
        out_specs=[VM] * (2 * n),
        scratch_shapes=[
            pltpu.VMEM((2, NG, ROWS, WID), BF),
            pltpu.VMEM((n, BLK, WID), BF),
            pltpu.VMEM((HEADS * BLK, SEQ), jnp.float32),
            pltpu.SemaphoreType.DMA,
        ],
        compiler_params=pltpu.CompilerParams(vmem_limit_bytes=24 << 20),
        name="tail",
        cost_estimate=pl.CostEstimate(
            flops=2 * n * BLK * D * WID + 4 * n * BLK * SEQ * WID,
            bytes_accessed=4 * D * WID,
            transcendentals=n * BLK * HEADS * SEQ,
        ),
    )(mod, pos, mask, tab, *o_all, q, k, v)


AXES = ("x", "zl", "c", "zh")


def pairs(step, x_core, only=None):
    out = []
    for x in range(4):
        for z in range(8):
            for c in range(2):
                if only is not None and c != only:
                    continue
                tx, tz = ((x + step) % 4, z) if c == x_core else (x, (z + step) % 8)
                out.append(
                    tuple(((i * 4 + (k & 3)) * 2 + c) * 2 + (k >> 2) for i, k in ((x, z), (tx, tz)))
                )
    return out


def send(a, step, x_core, only=None):
    return lax.ppermute(a, AXES, pairs(step, x_core, only))


def swap(a):
    return lax.ppermute(a, "c", [(0, 1), (1, 0)])


def gather_start(kv, q, o):
    own = jnp.concatenate([kv[:1], q, o, kv[1:]], axis=0)
    r1p, r1m = send(own, 1, 0), send(own, -1, 0)
    r2p, r2m = send(r1p[:5], 1, 0), send(r1m[1:], -1, 0)
    return own, r1p, r1m, r2p, r2m


def gather_kv(own, r1p, r1m, r2p, r2m):
    b = jnp.stack(
        [
            jnp.stack([own[0], r1p[0], r1m[0], r2p[0]]),
            jnp.stack([own[5], r1p[5], r1m[5], r2m[4]]),
        ]
    )
    t1p, t1m = send(b, 1, 1), send(b, -1, 1)
    t2p, t2m = send(t1p[0], 1, 1), send(t1m[1], -1, 1)
    return [b, t1p, t1m, t2p, t2m, swap(jnp.concatenate([b, t1p, t1m])), swap(jnp.stack([t2p, t2m]))]


def bundles(first, r3p, r3m, last, k):
    own, r1p, r1m, r2p, r2m = first
    b = jnp.stack([t[1 + k : 3 + k] for t in (own, r1p, r1m, r2p)])
    return b, jnp.stack([r2m[k : k + 2], r3p[k : k + 2], r3m[k : k + 2], last])


def gather_wide(b, b2, c):
    mine = c == 0
    t1p, t1m = send(b, 1, 1), send(b, -1, 1)
    t2p, t2m = send(jnp.where(mine, t1p, b2), 1, 1), send(jnp.where(mine, t1m, b2), -1, 1)
    t3p, t3m = send(jnp.where(mine, t2p, t1p), 1, 1), send(t2m, -1, 1)
    t4p, t4m = send(t3p[:2], 1, 1, 0), send(t3m[2:], -1, 1, 0)
    u = jnp.where(mine, jnp.concatenate([t4p, t4m]), b2)
    swaps = [swap(jnp.concatenate(t)) for t in ((b, t1p, t1m), (t2p, t2m), (t3p, t3m), (u,))]
    return [b, t1p, t1m, t2p, t2m, t3p, t3m, u] + swaps


def local(tokens, modality, block_mask, q_weight, kv_weight, o_weight):
    y, zh, c = lax.axis_index("y"), lax.axis_index("zh"), lax.axis_index("c")
    pos = jnp.stack([y, zh]).astype(jnp.int32)
    tab = piece_tables(lax.axis_index("x"), zh * 4 + lax.axis_index("zl"), c)
    tables = [jnp.asarray(t) for t in rotary_tables()]
    kv = lax.dynamic_slice_in_dim(kv_weight, y * (2 * HD), 2 * HD, 2)
    first = gather_start(kv, q_weight, jnp.swapaxes(o_weight, 1, 2))
    r2p, r2m = first[3:]
    r3p, r3m = send(r2p[1:], 1, 0, 1), send(r2m[:4], -1, 0, 1)
    r4p, r4m = send(r3p[:2], 1, 0, 1), send(r3m[2:], -1, 0, 1)
    kv_all = gather_kv(*first)
    q_all = gather_wide(*bundles(first, r3p, r3m, r4p, 0), c)
    o_all = gather_wide(*bundles(first, r3p, r3m, r4m, 2), c)
    small = (modality[0], pos, block_mask[0], tab)
    q, k, v, o2a, o2b = head(*small, kv_all, q_all, o_all, tokens[0], tables)
    up = [(i, (i + 1) % NY) for i in range(NY)]
    down = [(i, (i - 1) % NY) for i in range(NY)]
    f32 = jnp.float32

    def add(a, b):
        return (a.astype(f32) + b.astype(f32)).astype(BF)

    far_a, far_b = lax.ppermute(o2a, "y", up), lax.ppermute(o2b, "y", down)
    o1a, o1b, o3a, o3b = tail((1, 3), *small, o_all, q, k, v)
    pb, ma = lax.ppermute(o1b, "y", up), lax.ppermute(o3a, "y", down)
    pa, mb = add(o1a, far_a), add(o3b, far_b)
    q = lax.optimization_barrier((q, pa, mb))[0]
    pa, mb = lax.ppermute(pa, "y", up), lax.ppermute(mb, "y", down)
    o0a, o0b = tail((0,), *small, o_all, q, k, v)
    out_a = (o0a.astype(f32) + pa.astype(f32) + ma.astype(f32)).astype(BF)
    out_b = (o0b.astype(f32) + pb.astype(f32) + mb.astype(f32)).astype(BF)
    return jnp.concatenate([out_a, out_b], axis=1)[None]


def solution(mesh):
    fine = Mesh(mesh.devices.reshape(4, 4, 2, 4, 2), ("x", "zl", "c", "y", "zh"))
    dp = ("x", "zl", "c")
    mp = ("y", "zh")
    in_specs = (
        P(dp, None, None),
        P(dp, None),
        P(dp, None, None),
        P(None, dp, mp),
        P(None, dp, None),
        P(None, mp, dp),
    )
    return jax.shard_map(
        local, mesh=fine, in_specs=in_specs, out_specs=P(dp, mp, None), check_vma=False
    )
```

```python
import functools

import jax
import jax.numpy as jnp
import numpy as np
from jax import lax
from jax.experimental import pallas as pl
from jax.experimental.pallas import tpu as pltpu
from jax.sharding import Mesh
from jax.sharding import PartitionSpec as P

D = 3584
HD = 128
BLK = 128
NBLK = 8
SEQ = 1024
ROWS = 112
NG = 32
NY = 4
QB = 4
HEADS = 4
WID = HEADS * HD
ROPE_THETA = 1000000.0
NEG = -1e30
ANY = pl.BlockSpec(memory_space=pl.ANY)
SM = pl.BlockSpec(memory_space=pltpu.SMEM)


def rotary_tables():
    half = HD // 2
    freq = ROPE_THETA ** (-np.arange(half, dtype=np.float64) * 2.0 / HD)
    freq = np.concatenate([freq, freq])[None, :]
    fine = np.arange(BLK, dtype=np.float64)[:, None] * freq
    base = BLK * np.arange(NBLK, dtype=np.float64)[:, None] * freq
    return [np.asarray(t, np.float32) for t in (np.cos(fine), np.sin(fine), np.cos(base), np.sin(base))]


def block_tables(tables, b):
    cf, sf = tables[0][...], tables[1][...]
    cb, sb = tables[2][pl.ds(b, 1), :], tables[3][pl.ds(b, 1), :]
    sign = jnp.where(lax.broadcasted_iota(jnp.int32, (1, HD), 1) < HD // 2, -1.0, 1.0)
    return cb * cf - sb * sf, sign * (sb * cf + cb * sf)


def rotate(x, cos, sin):
    return x * cos + pltpu.roll(x, HD // 2, 1) * sin


DX = (0, -1, 1, 2)
DZ = (0, -1, 1, -2, 2, -3, 3, 4)
Q_AT, O_AT, KV_AT = 0, 64, 128


def piece_tables(x, z, c):
    cc = jnp.stack([c, 1 - c])[:, None, None]
    four, eight = np.array(DX), np.array(DZ)

    def group(dx, dz):
        zs = (z + dz) & 7
        return (((x + dx) & 3) * 4 + (zs & 3)) * 2 + cc, zs >> 2

    gq, hq = group(four[None, None, :], eight[None, :, None])
    go, ho = group(four[None, :, None], eight[None, None, :])
    gk, _ = group(four[None, :, None], four[None, None, :])
    parts = (gq * 2 + hq, go * 2 + ho, gk)
    return jnp.concatenate([t.reshape(-1) for t in parts]).astype(jnp.int32)


def fetch(tab, base, refs, w, sem):
    for ref in refs:

        def start(j, carry, ref=ref, base=base):
            at = tab[base + j]
            cols = pl.ds(pl.multiple_of((at & 1) * (2 * HD), 2 * HD), 2 * HD)
            pltpu.make_async_copy(ref.at[j], w.at[:, at >> 1, :, cols], sem).start()
            return carry

        lax.fori_loop(0, ref.shape[0], start, 0)
        base += ref.shape[0]


def attend(i, zh, mask, q, k, v, s):
    b = 2 * i + zh
    diff = lax.broadcasted_iota(jnp.int32, (BLK, BLK), 1) - lax.broadcasted_iota(
        jnp.int32, (BLK, BLK), 0
    )
    diff = jnp.concatenate([diff] * HEADS, axis=0)
    qq = q[i]
    for j in range(NBLK):
        mb = mask[b, j]
        off = jnp.where(mb == 1, 4096, jnp.where(mb == 2, BLK * (b - j), -4096))
        sj = lax.dot_general(
            qq,
            k[j * BLK : (j + 1) * BLK, :],
            (((1,), (1,)), ((), ())),
            preferred_element_type=jnp.float32,
        )
        s[:, j * BLK : (j + 1) * BLK] = jnp.where(diff <= off, sj, NEG)
    sv = s[...]
    p = jnp.exp((sv - jnp.max(sv, axis=1, keepdims=True)) * (HD**-0.5))
    total = jnp.sum(p, axis=1, keepdims=True)
    a = jnp.dot(p.astype(BF), v[...], preferred_element_type=jnp.float32) / total
    a = a.astype(BF)
    return jnp.concatenate([a[h * BLK : (h + 1) * BLK] for h in range(HEADS)], axis=1)


def project_out(a, w, sec, outs):
    quarter = D // 4
    for g in range(4):
        wt = w[sec, 8 * g : 8 * g + 8].reshape(quarter, WID)
        r = lax.dot_general(a, wt, (((1,), (1,)), ((), ())), preferred_element_type=jnp.float32)
        outs[g // 2][:, (g % 2) * quarter : (g % 2 + 1) * quarter] = r.astype(BF)


def head_body(mod, pos, mask, tab, *refs):
    kv_refs, q_refs, o_refs, x_hbm, tables = refs[:7], refs[7:20], refs[20:29], refs[29], refs[30:34]
    q, k, v = refs[34:37]
    outs = refs[37:39]
    x, wk, wq, wo, s, inv, xsem, ksem, qsem, osem = refs[39:]
    y0, zh = pos[0], pos[1]
    for a in range(4):

        def start(j, carry, a=a):
            at = [tab[KV_AT + n * 16 + a * 4 + j] for n in range(2)]
            if a < 3:
                pltpu.make_async_copy(kv_refs[a].at[:, j], wk.at[:, at[0]], ksem).start()
                src = kv_refs[5].at[pl.ds(2 * a, 2), j]
            else:
                for m in range(2):
                    pltpu.make_async_copy(kv_refs[3 + m].at[j], wk.at[m, at[0]], ksem).start()
                src = kv_refs[6].at[:, j]
            pltpu.make_async_copy(src, wk.at[:, at[1]], ksem).start()
            return carry

        lax.fori_loop(0, 4, start, 0)
    order = [2 * i + zh for i in range(QB)] + [2 * i + 1 - zh for i in range(QB)]
    kinds = [mod[b] for b in order]
    n1 = sum(kinds)
    h0 = (NBLK - n1 + 1) // 2
    passes = h0 + (n1 + 1) // 2
    for t in range(NBLK + 2):
        inv[t] = -1
    c0, c1 = 0, 0
    for n, (b, kind) in enumerate(zip(order, kinds)):
        inv[jnp.where(kind == 0, c0, 2 * h0 + c1)] = b
        c0, c1 = c0 + 1 - kind, c1 + kind
        if n == QB - 1:
            p0, p1 = (c0 + 1) // 2, (c1 + 1) // 2

    def block_copy(t):
        rows = pl.ds(pl.multiple_of(inv[t] * BLK, BLK), BLK)
        return pltpu.make_async_copy(x_hbm.at[rows], x.at[t], xsem.at[t])

    def start_x(t, carry):
        @pl.when(inv[t] >= 0)
        def _():
            block_copy(t).start()

        return carry

    lax.fori_loop(0, NBLK + 2, start_x, 0)
    fetch(tab, Q_AT, q_refs, wq, qsem)
    fetch(tab, O_AT, o_refs, wo, osem)
    pltpu.make_async_copy(wk, wk, ksem).wait()

    def project_kv(p, carry):
        sec = jnp.where(p >= h0, 1, 0)
        ids = [inv[2 * p + t] for t in range(2)]
        for t in range(2):

            @pl.when(ids[t] >= 0)
            def _():
                block_copy(2 * p + t).wait()

        lhs = x[pl.ds(2 * p, 2)].reshape(2 * BLK, D)
        y = jnp.dot(lhs, wk[sec].reshape(D, 2 * HD), preferred_element_type=jnp.float32)
        for t in range(2):

            @pl.when(ids[t] >= 0)
            def _():
                yt = y[t * BLK : (t + 1) * BLK]
                cos, sin = block_tables(tables, ids[t])
                rows = pl.ds(pl.multiple_of(ids[t] * BLK, BLK), BLK)
                k[rows, :] = rotate(yt[:, :HD], cos, sin).astype(BF)
                v[rows, :] = yt[:, HD:].astype(BF)

        return carry

    lax.fori_loop(0, passes, project_kv, 0)
    pltpu.make_async_copy(wq, wq, qsem).wait()

    def project_q(p, carry):
        sec = jnp.where(p >= p0, 1, 0)
        slot = jnp.where(p >= p0, 2 * (h0 + p - p0), 2 * p)
        lhs = x[pl.ds(slot, 2)].reshape(2 * BLK, D)
        y = jnp.dot(lhs, wq[sec].reshape(D, WID), preferred_element_type=jnp.float32)
        for t in range(2):
            b = inv[slot + t]

            @pl.when((b >= 0) & ((b & 1) == zh))
            def _():
                cos, sin = block_tables(tables, b)
                for h in range(HEADS):
                    yt = y[t * BLK : (t + 1) * BLK, h * HD : (h + 1) * HD]
                    q[b >> 1, h * BLK : (h + 1) * BLK, :] = rotate(yt, cos, sin).astype(BF)

        return carry

    lax.fori_loop(0, p0 + p1, project_q, 0)
    far = (y0 + 2) & 3
    a = attend(far, zh, mask, q, k, v, s)
    pltpu.make_async_copy(wo, wo, osem).wait()
    project_out(a, wo, mod[2 * far + zh], outs)


def tail_body(rels, mod, pos, mask, tab, *refs):
    o_refs, (q, k, v), outs, (wo, att, s, osem) = refs[:9], refs[9:12], refs[12:-4], refs[-4:]
    y0, zh = pos[0], pos[1]
    fetch(tab, O_AT, o_refs, wo, osem)

    def one(n, carry):
        att[n] = attend((y0 + rels[0] + 2 * n) & 3, zh, mask, q, k, v, s)
        return carry

    lax.fori_loop(0, len(rels), one, 0)
    pltpu.make_async_copy(wo, wo, osem).wait()
    for n, rel in enumerate(rels):
        project_out(att[n], wo, mod[2 * ((y0 + rel) & 3) + zh], outs[2 * n : 2 * n + 2])


VM = pl.BlockSpec(memory_space=pltpu.VMEM)
BF = jnp.bfloat16
HALF_BLOCK = jax.ShapeDtypeStruct((BLK, D // 2), BF)


def head(mod, pos, mask, tab, kv_all, q_all, o_all, x, tables):
    return pl.pallas_call(
        head_body,
        out_shape=[
            jax.ShapeDtypeStruct((QB, HEADS * BLK, HD), BF),
            jax.ShapeDtypeStruct((SEQ, HD), BF),
            jax.ShapeDtypeStruct((SEQ, HD), BF),
            HALF_BLOCK,
            HALF_BLOCK,
        ],
        in_specs=[SM] * 4 + [ANY] * 30 + [VM] * 4,
        out_specs=[VM] * 5,
        scratch_shapes=[
            pltpu.VMEM((NBLK + 2, BLK, D), BF),
            pltpu.VMEM((2, NG, ROWS, 2 * HD), BF),
            pltpu.VMEM((2, NG, ROWS, WID), BF),
            pltpu.VMEM((2, NG, ROWS, WID), BF),
            pltpu.VMEM((HEADS * BLK, SEQ), jnp.float32),
            pltpu.SMEM((NBLK + 2,), jnp.int32),
            pltpu.SemaphoreType.DMA((NBLK + 2,)),
            pltpu.SemaphoreType.DMA,
            pltpu.SemaphoreType.DMA,
            pltpu.SemaphoreType.DMA,
        ],
        name="head",
        cost_estimate=pl.CostEstimate(
            flops=2 * SEQ * D * 2 * HD + 2 * QB * BLK * D * WID,
            bytes_accessed=2 * SEQ * D + 8 * D * HD + 8 * D * WID,
            transcendentals=BLK * HEADS * SEQ,
        ),
    )(mod, pos, mask, tab, *kv_all, *q_all, *o_all, x, *tables)


def tail(rels, mod, pos, mask, tab, o_all, q, k, v):
    n = len(rels)
    return pl.pallas_call(
        functools.partial(tail_body, rels),
        out_shape=[HALF_BLOCK] * (2 * n),
        in_specs=[SM] * 4 + [ANY] * 9 + [VM] * 3,
        out_specs=[VM] * (2 * n),
        scratch_shapes=[
            pltpu.VMEM((2, NG, ROWS, WID), BF),
            pltpu.VMEM((n, BLK, WID), BF),
            pltpu.VMEM((HEADS * BLK, SEQ), jnp.float32),
            pltpu.SemaphoreType.DMA,
        ],
        name="tail",
        cost_estimate=pl.CostEstimate(
            flops=2 * n * BLK * D * WID + 4 * n * BLK * SEQ * WID,
            bytes_accessed=4 * D * WID,
            transcendentals=n * BLK * HEADS * SEQ,
        ),
    )(mod, pos, mask, tab, *o_all, q, k, v)


def along_x(a, step):
    return lax.ppermute(a, "x", [(i, (i + step) % 4) for i in range(4)])


def along_z(a, step):
    at = [(z & 3) * 2 + (z >> 2) for z in range(8)]
    return lax.ppermute(a, ("zl", "zh"), [(at[z], at[(z + step) % 8]) for z in range(8)])


def swap(a):
    return lax.ppermute(a, "c", [(0, 1), (1, 0)])


def gather(kv, q, o, tab):
    own = jnp.concatenate([kv[:1], o, kv[1:]], axis=0)
    p1p, p1m = along_x(q, 1), along_x(q, -1)
    r1p, r1m = along_z(own, 1), along_z(own, -1)
    r1p, tab = lax.optimization_barrier((r1p, tab))
    p2p, p2m = along_x(p1p[0], 1), along_x(p1m[1], -1)
    r2p, r2m = along_z(r1p[:3], 1), along_z(r1m[1:], -1)
    b = jnp.stack([q, p1p, p1m, jnp.stack([p2p, p2m])])
    t1p, t1m = along_z(b, 1), along_z(b, -1)
    t2p, t2m = along_z(t1p, 1), along_z(t1m, -1)
    t3p, t3m = along_z(t2p, 1), along_z(t2m, -1)
    t4p, t4m = along_z(t3p[:2], 1), along_z(t3m[2:], -1)
    q_all = [b, t1p, t1m, t2p, t2m, t3p, t3m, t4p, t4m]
    q_all += [swap(jnp.concatenate(t)) for t in ((b, t1p, t1m), (t2p, t2m), (t3p, t3m), (t4p, t4m))]
    b = jnp.stack(
        [
            jnp.stack([own[0], r1p[0], r1m[0], r2p[0]]),
            jnp.stack([own[3], r1p[3], r1m[3], r2m[2]]),
        ]
    )
    t1p, t1m = along_x(b, 1), along_x(b, -1)
    t2p, t2m = along_x(t1p[0], 1), along_x(t1m[1], -1)
    kv_all = [b, t1p, t1m, t2p, t2m, swap(jnp.concatenate([b, t1p, t1m])), swap(jnp.stack([t2p, t2m]))]
    r2p, r2m = r2p[1:], r2m[:2]
    r3p, r3m = along_z(r2p, 1), along_z(r2m, -1)
    r4 = jnp.stack([along_z(r3p[0], 1), along_z(r3m[1], -1)])
    b = jnp.stack([o, r1p[1:3], r1m[1:3], r2p, r2m, r3p, r3m, r4])
    t1p, t1m = along_x(b, 1), along_x(b, -1)
    t2p, t2m = along_x(t1p[:4], 1), along_x(t1m[4:], -1)
    o_all = [b, t1p, t1m, t2p, t2m, swap(b), swap(t1p), swap(t1m), swap(jnp.concatenate([t2p, t2m]))]
    return kv_all, q_all, o_all, tab


def local(tokens, modality, block_mask, q_weight, kv_weight, o_weight):
    y, zh, c = lax.axis_index("y"), lax.axis_index("zh"), lax.axis_index("c")
    pos = jnp.stack([y, zh]).astype(jnp.int32)
    tab = piece_tables(lax.axis_index("x"), zh * 4 + lax.axis_index("zl"), c)
    tables = [jnp.asarray(t) for t in rotary_tables()]
    kv = lax.dynamic_slice_in_dim(kv_weight, y * (2 * HD), 2 * HD, 2)
    kv_all, q_all, o_all, tab = gather(kv, q_weight, jnp.swapaxes(o_weight, 1, 2), tab)
    small = (modality[0], pos, block_mask[0], tab)
    q, k, v, o2a, o2b = head(*small, kv_all, q_all, o_all, tokens[0], tables)
    up = [(i, (i + 1) % NY) for i in range(NY)]
    down = [(i, (i - 1) % NY) for i in range(NY)]
    f32 = jnp.float32

    def add(a, b):
        return (a.astype(f32) + b.astype(f32)).astype(BF)

    far_a, far_b = lax.ppermute(o2a, "y", up), lax.ppermute(o2b, "y", down)
    o1a, o1b, o3a, o3b = tail((1, 3), *small, o_all, q, k, v)
    pb, ma = lax.ppermute(o1b, "y", up), lax.ppermute(o3a, "y", down)
    pa, mb = add(o1a, far_a), add(o3b, far_b)
    q = lax.optimization_barrier((q, pa, mb))[0]
    pa, mb = lax.ppermute(pa, "y", up), lax.ppermute(mb, "y", down)
    o0a, o0b = tail((0,), *small, o_all, q, k, v)
    out_a = (o0a.astype(f32) + pa.astype(f32) + ma.astype(f32)).astype(BF)
    out_b = (o0b.astype(f32) + pb.astype(f32) + mb.astype(f32)).astype(BF)
    return jnp.concatenate([out_a, out_b], axis=1)[None]


def solution(mesh):
    fine = Mesh(mesh.devices.reshape(4, 4, 2, 4, 2), ("x", "zl", "c", "y", "zh"))
    dp = ("x", "zl", "c")
    mp = ("y", "zh")
    in_specs = (
        P(dp, None, None),
        P(dp, None),
        P(dp, None, None),
        P(None, dp, mp),
        P(None, dp, None),
        P(None, mp, dp),
    )
    return jax.shard_map(
        local, mesh=fine, in_specs=in_specs, out_specs=P(dp, mp, None), check_vma=False
    )
```

```python
import functools

import jax
import jax.numpy as jnp
import numpy as np
from jax import lax
from jax.experimental import pallas as pl
from jax.experimental.pallas import tpu as pltpu
from jax.sharding import Mesh
from jax.sharding import PartitionSpec as P

D = 3584
HD = 128
BLK = 128
NBLK = 8
SEQ = 1024
ROWS = 112
NG = 32
NY = 4
QB = 4
HEADS = 4
WID = HEADS * HD
ROPE_THETA = 1000000.0
NEG = -1e30
ANY = pl.BlockSpec(memory_space=pl.ANY)
SM = pl.BlockSpec(memory_space=pltpu.SMEM)


def rotary_tables():
    half = HD // 2
    freq = ROPE_THETA ** (-np.arange(half, dtype=np.float64) * 2.0 / HD)
    freq = np.concatenate([freq, freq])[None, :]
    fine = np.arange(BLK, dtype=np.float64)[:, None] * freq
    base = BLK * np.arange(NBLK, dtype=np.float64)[:, None] * freq
    return [np.asarray(t, np.float32) for t in (np.cos(fine), np.sin(fine), np.cos(base), np.sin(base))]


def block_tables(tables, b):
    cf, sf = tables[0][...], tables[1][...]
    cb, sb = tables[2][pl.ds(b, 1), :], tables[3][pl.ds(b, 1), :]
    sign = jnp.where(lax.broadcasted_iota(jnp.int32, (1, HD), 1) < HD // 2, -1.0, 1.0)
    return cb * cf - sb * sf, sign * (sb * cf + cb * sf)


def rotate(x, cos, sin):
    return x * cos + pltpu.roll(x, HD // 2, 1) * sin


DX = (0, -1, 1, 2)
DZ = (0, -1, 1, -2, 2, -3, 3, 4)
Q_AT, O_AT, KV_AT, POS = 0, 64, 128, 160


def piece_tables(x, z, c, y):
    cc = jnp.stack([c, 1 - c])[:, None, None]
    four, eight = np.array(DX), np.array(DZ)

    def group(dx, dz):
        zs = (z + dz) & 7
        return (((x + dx) & 3) * 4 + (zs & 3)) * 2 + cc, zs >> 2

    gq, hq = group(four[None, None, :], eight[None, :, None])
    go, ho = group(four[None, :, None], eight[None, None, :])
    gk, _ = group(four[None, :, None], four[None, None, :])
    parts = (gq * 2 + hq, go * 2 + ho, gk)
    parts += (y, z >> 2)
    return jnp.concatenate([t.reshape(-1) for t in parts]).astype(jnp.int32)


def fetch(tab, base, refs, w, sem):
    for ref in refs:

        def start(j, carry, ref=ref, base=base):
            at = tab[base + j]
            cols = pl.ds(pl.multiple_of((at & 1) * (2 * HD), 2 * HD), 2 * HD)
            pltpu.make_async_copy(ref.at[j], w.at[:, at >> 1, :, cols], sem).start()
            return carry

        lax.fori_loop(0, ref.shape[0], start, 0)
        base += ref.shape[0]


def attend(i, zh, mask, q, k, v, s, out):
    b = 2 * i + zh
    diff = lax.broadcasted_iota(jnp.int32, (BLK, BLK), 1) - lax.broadcasted_iota(
        jnp.int32, (BLK, BLK), 0
    )
    diff = jnp.concatenate([diff, diff], axis=0)

    def heads(n, carry):
        qq = q[i, pl.ds(pl.multiple_of(n * 2 * BLK, 2 * BLK), 2 * BLK), :]
        for j in range(NBLK):
            mb = mask[b, j]
            off = jnp.where(mb == 1, 4096, jnp.where(mb == 2, BLK * (b - j), -4096))
            sj = lax.dot_general(
                qq,
                k[j * BLK : (j + 1) * BLK, :],
                (((1,), (1,)), ((), ())),
                preferred_element_type=jnp.float32,
            )
            s[:, j * BLK : (j + 1) * BLK] = jnp.where(diff <= off, sj, NEG)
        sv = s[...]
        p = jnp.exp((sv - jnp.max(sv, axis=1, keepdims=True)) * (HD**-0.5))
        total = jnp.sum(p, axis=1, keepdims=True)
        a = jnp.dot(p.astype(BF), v[...], preferred_element_type=jnp.float32) / total
        a = a.astype(BF)
        cols = pl.ds(pl.multiple_of(n * 2 * HD, 2 * HD), 2 * HD)
        out[:, cols] = jnp.concatenate([a[:BLK], a[BLK:]], axis=1)
        return carry

    lax.fori_loop(0, HEADS // 2, heads, 0)


def project_out(a, w, sec, out, first, count):
    quarter = D // 4

    def chunk(g, carry):
        wt = w[sec, pl.ds(pl.multiple_of(8 * (first + g), 8), 8)].reshape(quarter, WID)
        r = lax.dot_general(a, wt, (((1,), (1,)), ((), ())), preferred_element_type=jnp.float32)
        out[:, pl.ds(pl.multiple_of(g * quarter, BLK), quarter)] = r.astype(BF)
        return carry

    lax.fori_loop(0, count, chunk, 0)


def head_body(mod, mask, tab, *refs):
    kv_refs, q_refs, o_refs, x_hbm, tables = refs[:6], refs[6:17], refs[17:24], refs[24], refs[25:29]
    q, k, v = refs[29:32]
    outs = refs[32:34]
    x, wk, wq, wo, att, s, inv, xsem, ksem, qsem, osem = refs[34:]
    y0, zh = tab[POS], tab[POS + 1]
    for a in range(4):

        def start(j, carry, a=a):
            at = [tab[KV_AT + n * 16 + a * 4 + j] for n in range(2)]
            if a < 3:
                pltpu.make_async_copy(kv_refs[a].at[:, j], wk.at[:, at[0]], ksem).start()
            else:
                for m in range(2):
                    pltpu.make_async_copy(kv_refs[3 + m].at[j], wk.at[m, at[0]], ksem).start()
            src = kv_refs[5].at[pl.ds(2 * a, 2), j]
            pltpu.make_async_copy(src, wk.at[:, at[1]], ksem).start()
            return carry

        lax.fori_loop(0, 4, start, 0)
    order = [2 * i + zh for i in range(QB)] + [2 * i + 1 - zh for i in range(QB)]
    kinds = [mod[b] for b in order]
    n1 = sum(kinds)
    h0 = (NBLK - n1 + 1) // 2
    passes = h0 + (n1 + 1) // 2
    for t in range(NBLK + 2):
        inv[t] = -1
    c0, c1 = 0, 0
    for n, (b, kind) in enumerate(zip(order, kinds)):
        inv[jnp.where(kind == 0, c0, 2 * h0 + c1)] = b
        c0, c1 = c0 + 1 - kind, c1 + kind
        if n == QB - 1:
            p0, p1 = (c0 + 1) // 2, (c1 + 1) // 2

    def block_copy(t):
        rows = pl.ds(pl.multiple_of(inv[t] * BLK, BLK), BLK)
        return pltpu.make_async_copy(x_hbm.at[rows], x.at[t], xsem.at[t])

    def start_x(t, carry):
        @pl.when(inv[t] >= 0)
        def _():
            block_copy(t).start()

        return carry

    lax.fori_loop(0, NBLK + 2, start_x, 0)
    fetch(tab, Q_AT, q_refs, wq, qsem)
    fetch(tab, O_AT, o_refs, wo, osem)
    pltpu.make_async_copy(wk, wk, ksem).wait()

    def project_kv(p, carry):
        sec = jnp.where(p >= h0, 1, 0)
        ids = [inv[2 * p + t] for t in range(2)]
        for t in range(2):

            @pl.when(ids[t] >= 0)
            def _():
                block_copy(2 * p + t).wait()

        lhs = x[pl.ds(2 * p, 2)].reshape(2 * BLK, D)
        y = jnp.dot(lhs, wk[sec].reshape(D, 2 * HD), preferred_element_type=jnp.float32)
        for t in range(2):

            @pl.when(ids[t] >= 0)
            def _():
                yt = y[t * BLK : (t + 1) * BLK]
                cos, sin = block_tables(tables, ids[t])
                rows = pl.ds(pl.multiple_of(ids[t] * BLK, BLK), BLK)
                k[rows, :] = rotate(yt[:, :HD], cos, sin).astype(BF)
                v[rows, :] = yt[:, HD:].astype(BF)

        return carry

    lax.fori_loop(0, passes, project_kv, 0)
    pltpu.make_async_copy(wq, wq, qsem).wait()

    def project_q(p, carry):
        sec = jnp.where(p >= p0, 1, 0)
        slot = jnp.where(p >= p0, 2 * (h0 + p - p0), 2 * p)
        lhs = x[pl.ds(slot, 2)].reshape(2 * BLK, D)
        y = jnp.dot(lhs, wq[sec].reshape(D, WID), preferred_element_type=jnp.float32)
        for t in range(2):
            b = inv[slot + t]

            @pl.when((b >= 0) & ((b & 1) == zh))
            def _():
                cos, sin = block_tables(tables, b)
                for h in range(HEADS):
                    yt = y[t * BLK : (t + 1) * BLK, h * HD : (h + 1) * HD]
                    q[b >> 1, h * BLK : (h + 1) * BLK, :] = rotate(yt, cos, sin).astype(BF)

        return carry

    lax.fori_loop(0, p0 + p1, project_q, 0)
    far = (y0 + 2) & 3
    attend(far, zh, mask, q, k, v, s, att)
    pltpu.make_async_copy(wo, wo, osem).wait()
    for n in range(2):
        project_out(att[...], wo, mod[2 * far + zh], outs[n], 2 * n, 2)


def tail_body(mod, mask, tab, *refs):
    o_refs, (q, k, v, out, wo, att, s, osem) = refs[:7], refs[7:]
    y0, zh = tab[POS], tab[POS + 1]
    fetch(tab, O_AT, o_refs, wo, osem)

    def one(n, carry):
        attend((y0 + 3 + n) & 3, zh, mask, q, k, v, s, att.at[n])
        return carry

    lax.fori_loop(0, 3, one, 0)
    pltpu.make_async_copy(wo, wo, osem).wait()

    def two(n, carry):
        project_out(att[n], wo, mod[2 * ((y0 + 3 + n) & 3) + zh], out.at[n], 0, 4)
        return carry

    lax.fori_loop(0, 3, two, 0)


VM = pl.BlockSpec(memory_space=pltpu.VMEM)
BF = jnp.bfloat16
HALF_BLOCK = jax.ShapeDtypeStruct((BLK, D // 2), BF)


def head(mod, mask, tab, kv_all, q_all, o_all, x, tables):
    return pl.pallas_call(
        head_body,
        out_shape=[
            jax.ShapeDtypeStruct((QB, HEADS * BLK, HD), BF),
            jax.ShapeDtypeStruct((SEQ, HD), BF),
            jax.ShapeDtypeStruct((SEQ, HD), BF),
            HALF_BLOCK,
            HALF_BLOCK,
        ],
        in_specs=[SM] * 3 + [ANY] * 25 + [VM] * 4,
        out_specs=[VM] * 5,
        scratch_shapes=[
            pltpu.VMEM((NBLK + 2, BLK, D), BF),
            pltpu.VMEM((2, NG, ROWS, 2 * HD), BF),
            pltpu.VMEM((2, NG, ROWS, WID), BF),
            pltpu.VMEM((2, NG, ROWS, WID), BF),
            pltpu.VMEM((BLK, WID), BF),
            pltpu.VMEM((2 * BLK, SEQ), jnp.float32),
            pltpu.SMEM((NBLK + 2,), jnp.int32),
            pltpu.SemaphoreType.DMA((NBLK + 2,)),
            pltpu.SemaphoreType.DMA,
            pltpu.SemaphoreType.DMA,
            pltpu.SemaphoreType.DMA,
        ],
        name="head",
        cost_estimate=pl.CostEstimate(
            flops=2 * SEQ * D * 2 * HD + 2 * QB * BLK * D * WID,
            bytes_accessed=2 * SEQ * D + 8 * D * HD + 8 * D * WID,
            transcendentals=BLK * HEADS * SEQ,
        ),
    )(mod, mask, tab, *kv_all, *q_all, *o_all, x, *tables)


def tail(mod, mask, tab, o_all, q, k, v):
    return pl.pallas_call(
        tail_body,
        out_shape=jax.ShapeDtypeStruct((3, BLK, D), BF),
        in_specs=[SM] * 3 + [ANY] * 7 + [VM] * 3,
        out_specs=VM,
        scratch_shapes=[
            pltpu.VMEM((2, NG, ROWS, WID), BF),
            pltpu.VMEM((3, BLK, WID), BF),
            pltpu.VMEM((2 * BLK, SEQ), jnp.float32),
            pltpu.SemaphoreType.DMA,
        ],
        name="tail",
        cost_estimate=pl.CostEstimate(
            flops=6 * BLK * D * WID + 12 * BLK * SEQ * WID,
            bytes_accessed=4 * D * WID,
            transcendentals=3 * BLK * HEADS * SEQ,
        ),
    )(mod, mask, tab, *o_all, q, k, v)


def along_x(a, step):
    return lax.ppermute(a, "x", [(i, (i + step) % 4) for i in range(4)])


def along_z(a, step):
    at = [(z & 3) * 2 + (z >> 2) for z in range(8)]
    return lax.ppermute(a, ("zl", "zh"), [(at[z], at[(z + step) % 8]) for z in range(8)])


def swap(a):
    return lax.ppermute(a, "c", [(0, 1), (1, 0)])


def gather(kv, q, o, tab):
    own = jnp.concatenate([kv[:1], o, kv[1:]], axis=0)
    p1p, p1m = along_x(q, 1), along_x(q, -1)
    r1p, r1m = along_z(own, 1), along_z(own, -1)
    p2p, p2m = along_x(p1p[0], 1), along_x(p1m[1], -1)
    r2p, r2m = along_z(r1p[:3], 1), along_z(r1m[1:], -1)
    kb = jnp.stack(
        [
            jnp.stack([own[0], r1p[0], r1m[0], r2p[0]]),
            jnp.stack([own[3], r1p[3], r1m[3], r2m[2]]),
        ]
    )
    k1p, k1m = along_x(kb, 1), along_x(kb, -1)
    b = jnp.stack([q, p1p, p1m, jnp.stack([p2p, p2m])])
    b, r2p, r2m = lax.optimization_barrier((b, r2p[1:], r2m[:2]))
    r3p, r3m = along_z(r2p, 1), along_z(r2m, -1)
    t1p, t1m = along_z(b, 1), along_z(b, -1)
    r4 = jnp.stack([along_z(r3p[0], 1), along_z(r3m[1], -1)])
    t1p, t1m, r4, k1p, k1m, tab = lax.optimization_barrier((t1p, t1m, r4, k1p, k1m, tab))
    ob = jnp.stack([o, r1p[1:3], r1m[1:3], r2p, r2m, r3p, r3m, r4])
    o1p, o1m = along_x(ob, 1), along_x(ob, -1)
    t2p, t2m = along_z(t1p, 1), along_z(t1m, -1)
    k2p, k2m = along_x(k1p[0], 1), along_x(k1m[1], -1)
    kv_all = [kb, k1p, k1m, k2p, k2m, swap(jnp.concatenate([kb, k1p, k1m, jnp.stack([k2p, k2m])]))]
    t3p, t3m = along_z(t2p, 1), along_z(t2m, -1)
    o1p, o1m, t3p, t3m = lax.optimization_barrier((o1p, o1m, t3p, t3m))
    t4p, t4m = along_z(t3p[:2], 1), along_z(t3m[2:], -1)
    o2p, o2m = along_x(o1p[:4], 1), along_x(o1m[4:], -1)
    q_all = [b, t1p, t1m, t2p, t2m, t3p, t3m, t4p, t4m]
    q_all += [swap(jnp.concatenate(t)) for t in ((b, t1p, t1m, t2p, t2m), (t3p, t3m, t4p, t4m))]
    o_all = [ob, o1p, o1m, o2p, o2m]
    o_all += [swap(jnp.concatenate(t)) for t in ((ob, o1p, o1m), (o2p, o2m))]
    return kv_all, q_all, o_all, tab


def local(tokens, modality, block_mask, q_weight, kv_weight, o_weight):
    y, zh, c = lax.axis_index("y"), lax.axis_index("zh"), lax.axis_index("c")
    tab = piece_tables(lax.axis_index("x"), zh * 4 + lax.axis_index("zl"), c, y)
    tables = [jnp.asarray(t) for t in rotary_tables()]
    kv = lax.dynamic_slice_in_dim(kv_weight, y * (2 * HD), 2 * HD, 2)
    kv_all, q_all, o_all, tab = gather(kv, q_weight, jnp.swapaxes(o_weight, 1, 2), tab)
    small = (modality[0], block_mask[0], tab)
    q, k, v, o2a, o2b = head(*small, kv_all, q_all, o_all, tokens[0], tables)
    up = [(i, (i + 1) % NY) for i in range(NY)]
    down = [(i, (i - 1) % NY) for i in range(NY)]
    f32, half = jnp.float32, D // 2

    def add(a, b):
        return (a.astype(f32) + b.astype(f32)).astype(BF)

    far_a, far_b = lax.ppermute(o2a, "y", up), lax.ppermute(o2b, "y", down)
    o3, o0, o1 = tail(*small, o_all, q, k, v)
    p = jnp.concatenate([add(o1[:, :half], far_a), o1[:, half:]], axis=1)
    m = jnp.concatenate([o3[:, :half], add(o3[:, half:], far_b)], axis=1)
    p, m = lax.ppermute(p, "y", up), lax.ppermute(m, "y", down)
    return (o0.astype(f32) + p.astype(f32) + m.astype(f32)).astype(BF)[None]


def solution(mesh):
    fine = Mesh(mesh.devices.reshape(4, 4, 2, 4, 2), ("x", "zl", "c", "y", "zh"))
    dp = ("x", "zl", "c")
    mp = ("y", "zh")
    in_specs = (
        P(dp, None, None),
        P(dp, None),
        P(dp, None, None),
        P(None, dp, mp),
        P(None, dp, None),
        P(None, mp, dp),
    )
    return jax.shard_map(
        local, mesh=fine, in_specs=in_specs, out_specs=P(dp, mp, None), check_vma=False
    )
```

```python
import functools

import jax
import jax.numpy as jnp
import numpy as np
from jax import lax
from jax.experimental import pallas as pl
from jax.experimental.pallas import tpu as pltpu
from jax.sharding import Mesh
from jax.sharding import PartitionSpec as P

D = 3584
HD = 128
BLK = 128
NBLK = 8
SEQ = 1024
ROWS = 112
NG = 32
NY = 4
QB = 4
HEADS = 4
WID = HEADS * HD
ROPE_THETA = 1000000.0
NEG = -1e30
ANY = pl.BlockSpec(memory_space=pl.ANY)
SM = pl.BlockSpec(memory_space=pltpu.SMEM)


def rotary_tables():
    half = HD // 2
    freq = ROPE_THETA ** (-np.arange(half, dtype=np.float64) * 2.0 / HD)
    freq = np.concatenate([freq, freq])[None, :]
    fine = np.arange(BLK, dtype=np.float64)[:, None] * freq
    base = BLK * np.arange(NBLK, dtype=np.float64)[:, None] * freq
    return [np.asarray(t, np.float32) for t in (np.cos(fine), np.sin(fine), np.cos(base), np.sin(base))]


def block_tables(tables, b):
    cf, sf = tables[0][...], tables[1][...]
    cb, sb = tables[2][pl.ds(b, 1), :], tables[3][pl.ds(b, 1), :]
    sign = jnp.where(lax.broadcasted_iota(jnp.int32, (1, HD), 1) < HD // 2, -1.0, 1.0)
    return cb * cf - sb * sf, sign * (sb * cf + cb * sf)


def rotate(x, cos, sin):
    return x * cos + pltpu.roll(x, HD // 2, 1) * sin


DX = (0, -1, 1, 2)
DZ = (0, -1, 1, -2, 2, -3, 3, 4)
Q_AT, O_AT, KV_AT, POS = 0, 64, 128, 160


def piece_tables(x, z, c, y):
    cc = jnp.stack([c, 1 - c])[:, None, None]
    four, eight = np.array(DX), np.array(DZ)

    def group(dx, dz):
        zs = (z + dz) & 7
        return (((x + dx) & 3) * 4 + (zs & 3)) * 2 + cc, zs >> 2

    gq, hq = group(four[None, None, :], eight[None, :, None])
    go, ho = group(four[None, :, None], eight[None, None, :])
    gk, _ = group(four[None, :, None], four[None, None, :])
    parts = (gq * 2 + hq, go * 2 + ho, gk)
    parts += (y, z >> 2)
    return jnp.concatenate([t.reshape(-1) for t in parts]).astype(jnp.int32)


def fetch(tab, base, refs, w, sem):
    for ref in refs:

        def start(j, carry, ref=ref, base=base):
            at = tab[base + j]
            cols = pl.ds(pl.multiple_of((at & 1) * (2 * HD), 2 * HD), 2 * HD)
            pltpu.make_async_copy(ref.at[j], w.at[:, at >> 1, :, cols], sem).start()
            return carry

        lax.fori_loop(0, ref.shape[0], start, 0)
        base += ref.shape[0]


def attend(i, zh, mask, q, k, v, s, out):
    b = 2 * i + zh
    diff = lax.broadcasted_iota(jnp.int32, (BLK, BLK), 1) - lax.broadcasted_iota(
        jnp.int32, (BLK, BLK), 0
    )
    diff = jnp.concatenate([diff, diff], axis=0)

    def heads(n, carry):
        qq = q[i, pl.ds(pl.multiple_of(n * 2 * BLK, 2 * BLK), 2 * BLK), :]
        for j in range(NBLK):
            mb = mask[b, j]
            off = jnp.where(mb == 1, 4096, jnp.where(mb == 2, BLK * (b - j), -4096))
            sj = lax.dot_general(
                qq,
                k[j * BLK : (j + 1) * BLK, :],
                (((1,), (1,)), ((), ())),
                preferred_element_type=jnp.float32,
            )
            s[:, j * BLK : (j + 1) * BLK] = jnp.where(diff <= off, sj, NEG)
        sv = s[...]
        p = jnp.exp((sv - jnp.max(sv, axis=1, keepdims=True)) * (HD**-0.5))
        total = jnp.sum(p, axis=1, keepdims=True)
        a = jnp.dot(p.astype(BF), v[...], preferred_element_type=jnp.float32) / total
        a = a.astype(BF)
        cols = pl.ds(pl.multiple_of(n * 2 * HD, 2 * HD), 2 * HD)
        out[:, cols] = jnp.concatenate([a[:BLK], a[BLK:]], axis=1)
        return carry

    lax.fori_loop(0, HEADS // 2, heads, 0)


def project_out(a, w, sec, out, first, count):
    quarter = D // 4

    def chunk(g, carry):
        wt = w[sec, pl.ds(pl.multiple_of(8 * (first + g), 8), 8)].reshape(quarter, WID)
        r = lax.dot_general(a, wt, (((1,), (1,)), ((), ())), preferred_element_type=jnp.float32)
        out[:, pl.ds(pl.multiple_of(g * quarter, BLK), quarter)] = r.astype(BF)
        return carry

    lax.fori_loop(0, count, chunk, 0)


def head_body(mod, mask, tab, *refs):
    kv_refs, q_refs, o_refs, x_hbm, tables = refs[:6], refs[6:17], refs[17:24], refs[24], refs[25:29]
    q, k, v = refs[29:32]
    outs = refs[32:34]
    x, wk, wq, wo, att, s, inv, xsem, ksem, qsem, osem = refs[34:]
    y0, zh = tab[POS], tab[POS + 1]
    for a in range(4):

        def start(j, carry, a=a):
            at = [tab[KV_AT + n * 16 + a * 4 + j] for n in range(2)]
            if a < 3:
                pltpu.make_async_copy(kv_refs[a].at[:, j], wk.at[:, at[0]], ksem).start()
            else:
                for m in range(2):
                    pltpu.make_async_copy(kv_refs[3 + m].at[j], wk.at[m, at[0]], ksem).start()
            src = kv_refs[5].at[pl.ds(2 * a, 2), j]
            pltpu.make_async_copy(src, wk.at[:, at[1]], ksem).start()
            return carry

        lax.fori_loop(0, 4, start, 0)
    order = [2 * i + zh for i in range(QB)] + [2 * i + 1 - zh for i in range(QB)]
    kinds = [mod[b] for b in order]
    n1 = sum(kinds)
    h0 = (NBLK - n1 + 1) // 2
    passes = h0 + (n1 + 1) // 2
    for t in range(NBLK + 2):
        inv[t] = -1
    c0, c1 = 0, 0
    for n, (b, kind) in enumerate(zip(order, kinds)):
        inv[jnp.where(kind == 0, c0, 2 * h0 + c1)] = b
        c0, c1 = c0 + 1 - kind, c1 + kind
        if n == QB - 1:
            p0, p1 = (c0 + 1) // 2, (c1 + 1) // 2

    def block_copy(t):
        rows = pl.ds(pl.multiple_of(inv[t] * BLK, BLK), BLK)
        return pltpu.make_async_copy(x_hbm.at[rows], x.at[t], xsem.at[t])

    def start_x(t, carry):
        @pl.when(inv[t] >= 0)
        def _():
            block_copy(t).start()

        return carry

    lax.fori_loop(0, NBLK + 2, start_x, 0)
    fetch(tab, Q_AT, q_refs, wq, qsem)
    fetch(tab, O_AT, o_refs, wo, osem)
    pltpu.make_async_copy(wk, wk, ksem).wait()

    def project_kv(p, carry):
        sec = jnp.where(p >= h0, 1, 0)
        ids = [inv[2 * p + t] for t in range(2)]
        for t in range(2):

            @pl.when(ids[t] >= 0)
            def _():
                block_copy(2 * p + t).wait()

        lhs = x[pl.ds(2 * p, 2)].reshape(2 * BLK, D)
        y = jnp.dot(lhs, wk[sec].reshape(D, 2 * HD), preferred_element_type=jnp.float32)
        for t in range(2):

            @pl.when(ids[t] >= 0)
            def _():
                yt = y[t * BLK : (t + 1) * BLK]
                cos, sin = block_tables(tables, ids[t])
                rows = pl.ds(pl.multiple_of(ids[t] * BLK, BLK), BLK)
                k[rows, :] = rotate(yt[:, :HD], cos, sin).astype(BF)
                v[rows, :] = yt[:, HD:].astype(BF)

        return carry

    lax.fori_loop(0, passes, project_kv, 0)
    pltpu.make_async_copy(wq, wq, qsem).wait()

    def project_q(p, carry):
        sec = jnp.where(p >= p0, 1, 0)
        slot = jnp.where(p >= p0, 2 * (h0 + p - p0), 2 * p)
        lhs = x[pl.ds(slot, 2)].reshape(2 * BLK, D)
        y = jnp.dot(lhs, wq[sec].reshape(D, WID), preferred_element_type=jnp.float32)
        for t in range(2):
            b = inv[slot + t]

            @pl.when((b >= 0) & ((b & 1) == zh))
            def _():
                cos, sin = block_tables(tables, b)
                for h in range(HEADS):
                    yt = y[t * BLK : (t + 1) * BLK, h * HD : (h + 1) * HD]
                    q[b >> 1, h * BLK : (h + 1) * BLK, :] = rotate(yt, cos, sin).astype(BF)

        return carry

    lax.fori_loop(0, p0 + p1, project_q, 0)
    far = (y0 + 2) & 3
    attend(far, zh, mask, q, k, v, s, att)
    pltpu.make_async_copy(wo, wo, osem).wait()
    for n in range(2):
        project_out(att[...], wo, mod[2 * far + zh], outs[n], 2 * n, 2)


def tail_body(first, count, mod, mask, tab, *refs):
    o_refs, (q, k, v, out, wo, att, s, osem) = refs[:7], refs[7:]
    y0, zh = tab[POS], tab[POS + 1]
    fetch(tab, O_AT, o_refs, wo, osem)

    def one(n, carry):
        attend((y0 + first + 2 * n) & 3, zh, mask, q, k, v, s, att.at[n])
        return carry

    lax.fori_loop(0, count, one, 0)
    pltpu.make_async_copy(wo, wo, osem).wait()

    def two(n, carry):
        sec = mod[2 * ((y0 + first + 2 * n) & 3) + zh]
        project_out(att[n], wo, sec, out.at[n], 0, 4)
        return carry

    lax.fori_loop(0, count, two, 0)


VM = pl.BlockSpec(memory_space=pltpu.VMEM)
BF = jnp.bfloat16
HALF_BLOCK = jax.ShapeDtypeStruct((BLK, D // 2), BF)


def head(mod, mask, tab, kv_all, q_all, o_all, x, tables):
    return pl.pallas_call(
        head_body,
        out_shape=[
            jax.ShapeDtypeStruct((QB, HEADS * BLK, HD), BF),
            jax.ShapeDtypeStruct((SEQ, HD), BF),
            jax.ShapeDtypeStruct((SEQ, HD), BF),
            HALF_BLOCK,
            HALF_BLOCK,
        ],
        in_specs=[SM] * 3 + [ANY] * 25 + [VM] * 4,
        out_specs=[VM] * 5,
        scratch_shapes=[
            pltpu.VMEM((NBLK + 2, BLK, D), BF),
            pltpu.VMEM((2, NG, ROWS, 2 * HD), BF),
            pltpu.VMEM((2, NG, ROWS, WID), BF),
            pltpu.VMEM((2, NG, ROWS, WID), BF),
            pltpu.VMEM((BLK, WID), BF),
            pltpu.VMEM((2 * BLK, SEQ), jnp.float32),
            pltpu.SMEM((NBLK + 2,), jnp.int32),
            pltpu.SemaphoreType.DMA((NBLK + 2,)),
            pltpu.SemaphoreType.DMA,
            pltpu.SemaphoreType.DMA,
            pltpu.SemaphoreType.DMA,
        ],
        name="head",
        cost_estimate=pl.CostEstimate(
            flops=2 * SEQ * D * 2 * HD + 2 * QB * BLK * D * WID,
            bytes_accessed=2 * SEQ * D + 8 * D * HD + 8 * D * WID,
            transcendentals=BLK * HEADS * SEQ,
        ),
    )(mod, mask, tab, *kv_all, *q_all, *o_all, x, *tables)


def tail(first, count, mod, mask, tab, o_all, q, k, v):
    return pl.pallas_call(
        functools.partial(tail_body, first, count),
        out_shape=jax.ShapeDtypeStruct((count, BLK, D), BF),
        in_specs=[SM] * 3 + [ANY] * 7 + [VM] * 3,
        out_specs=VM,
        scratch_shapes=[
            pltpu.VMEM((2, NG, ROWS, WID), BF),
            pltpu.VMEM((count, BLK, WID), BF),
            pltpu.VMEM((2 * BLK, SEQ), jnp.float32),
            pltpu.SemaphoreType.DMA,
        ],
        name="tail",
        cost_estimate=pl.CostEstimate(
            flops=count * (2 * BLK * D * WID + 4 * BLK * SEQ * WID),
            bytes_accessed=4 * D * WID,
            transcendentals=count * BLK * HEADS * SEQ,
        ),
    )(mod, mask, tab, *o_all, q, k, v)


def along_x(a, step):
    return lax.ppermute(a, "x", [(i, (i + step) % 4) for i in range(4)])


def along_z(a, step):
    at = [(z & 3) * 2 + (z >> 2) for z in range(8)]
    return lax.ppermute(a, ("zl", "zh"), [(at[z], at[(z + step) % 8]) for z in range(8)])


def swap(a):
    return lax.ppermute(a, "c", [(0, 1), (1, 0)])


def gather(kv, q, o, at):
    p1p, p1m = along_x(q, 1), along_x(q, -1)
    own = jnp.concatenate([kv[:1], o, kv[1:]], axis=0)
    r1p, r1m = along_z(own, 1), along_z(own, -1)
    p2p, p2m = along_x(p1p[0], 1), along_x(p1m[1], -1)
    r2p, r2m = along_z(r1p[:3], 1), along_z(r1m[1:], -1)
    kb = jnp.stack(
        [
            jnp.stack([own[0], r1p[0], r1m[0], r2p[0]]),
            jnp.stack([own[3], r1p[3], r1m[3], r2m[2]]),
        ]
    )
    k1p, k1m = along_x(kb, 1), along_x(kb, -1)
    r2p, r2m = r2p[1:], r2m[:2]
    r3p, r3m = along_z(r2p, 1), along_z(r2m, -1)
    b = jnp.stack([q, p1p, p1m, jnp.stack([p2p, p2m])])
    b, r3p, r3m = lax.optimization_barrier((b, r3p, r3m))
    r4 = jnp.stack([along_z(r3p[0], 1), along_z(r3m[1], -1)])
    t1p, t1m = along_z(b, 1), along_z(b, -1)
    t1p, t1m, r4, k1p, k1m = lax.optimization_barrier((t1p, t1m, r4, k1p, k1m))
    ob = jnp.stack([o, r1p[1:3], r1m[1:3], r2p, r2m, r3p, r3m, r4])
    o1p, o1m = along_x(ob, 1), along_x(ob, -1)
    t2p, t2m = along_z(t1p, 1), along_z(t1m, -1)
    k2p, k2m = along_x(k1p[0], 1), along_x(k1m[1], -1)
    kv_all = [kb, k1p, k1m, k2p, k2m]
    kv_all.append(swap(jnp.concatenate([kb, k1p, k1m, jnp.stack([k2p, k2m])])))
    t2p, t2m, at = lax.optimization_barrier((t2p, t2m, at))
    tab = piece_tables(*at)
    t3p, t3m = along_z(t2p, 1), along_z(t2m, -1)
    o1p, o1m, t3p, t3m = lax.optimization_barrier((o1p, o1m, t3p, t3m))
    o2p, o2m = along_x(o1p[:4], 1), along_x(o1m[4:], -1)
    t4p, t4m = along_z(t3p[:2], 1), along_z(t3m[2:], -1)
    q_all = [b, t1p, t1m, t2p, t2m, t3p, t3m, t4p, t4m]
    q_all.append(swap(jnp.concatenate([b, t1p, t1m, t2p, t2m])))
    q_all.append(swap(jnp.concatenate([t3p, t3m, t4p, t4m])))
    o_all = [ob, o1p, o1m, o2p, o2m]
    o_all.append(swap(jnp.concatenate([ob, o1p, o1m])))
    o_all.append(swap(jnp.concatenate([o2p, o2m])))
    return kv_all, q_all, o_all, tab


def local(tokens, modality, block_mask, q_weight, kv_weight, o_weight):
    y, zh, c = lax.axis_index("y"), lax.axis_index("zh"), lax.axis_index("c")
    at = (lax.axis_index("x"), zh * 4 + lax.axis_index("zl"), c, y)
    tables = [jnp.asarray(t) for t in rotary_tables()]
    kv = lax.dynamic_slice_in_dim(kv_weight, y * (2 * HD), 2 * HD, 2)
    kv_all, q_all, o_all, tab = gather(kv, q_weight, jnp.swapaxes(o_weight, 1, 2), at)
    small = (modality[0], block_mask[0], tab)
    q, k, v, o2a, o2b = head(*small, kv_all, q_all, o_all, tokens[0], tables)
    up = [(i, (i + 1) % NY) for i in range(NY)]
    down = [(i, (i - 1) % NY) for i in range(NY)]
    f32, half = jnp.float32, D // 2

    def add(a, b):
        return (a.astype(f32) + b.astype(f32)).astype(BF)

    far_a = lax.ppermute(o2a, "y", up)
    far_b = lax.ppermute(o2b, "y", down)
    o3, o1 = tail(3, 2, *small, o_all, q, k, v)
    p = jnp.concatenate([add(o1[:, :half], far_a), o1[:, half:]], axis=1)
    m = jnp.concatenate([o3[:, :half], add(o3[:, half:], far_b)], axis=1)
    p = lax.ppermute(p, "y", up)
    m = lax.ppermute(m, "y", down)
    o0 = tail(0, 1, *small, o_all, q, k, v)[0]
    return (o0.astype(f32) + p.astype(f32) + m.astype(f32)).astype(BF)[None]


def solution(mesh):
    fine = Mesh(mesh.devices.reshape(4, 4, 2, 4, 2), ("x", "zl", "c", "y", "zh"))
    dp = ("x", "zl", "c")
    mp = ("y", "zh")
    in_specs = (
        P(dp, None, None),
        P(dp, None),
        P(dp, None, None),
        P(None, dp, mp),
        P(None, dp, None),
        P(None, mp, dp),
    )
    return jax.shard_map(local, mesh=fine, in_specs=in_specs, out_specs=P(dp, mp, None), check_vma=False)
```

```python
import functools

import jax
import jax.numpy as jnp
import numpy as np
from jax import lax
from jax.experimental import pallas as pl
from jax.experimental.pallas import tpu as pltpu
from jax.sharding import Mesh
from jax.sharding import PartitionSpec as P

D = 3584
HD = 128
BLK = 128
NBLK = 8
SEQ = 1024
ROWS = 112
NG = 32
NY = 4
QB = 4
HEADS = 4
WID = HEADS * HD
ROPE_THETA = 1000000.0
NEG = -1e30
ANY = pl.BlockSpec(memory_space=pl.ANY)
SM = pl.BlockSpec(memory_space=pltpu.SMEM)


def rotary_tables():
    half = HD // 2
    freq = ROPE_THETA ** (-np.arange(half, dtype=np.float64) * 2.0 / HD)
    freq = np.concatenate([freq, freq])[None, :]
    fine = np.arange(BLK, dtype=np.float64)[:, None] * freq
    base = BLK * np.arange(NBLK, dtype=np.float64)[:, None] * freq
    return [np.asarray(t, np.float32) for t in (np.cos(fine), np.sin(fine), np.cos(base), np.sin(base))]


def block_tables(tables, b):
    cf, sf = tables[0][...], tables[1][...]
    cb, sb = tables[2][pl.ds(b, 1), :], tables[3][pl.ds(b, 1), :]
    sign = jnp.where(lax.broadcasted_iota(jnp.int32, (1, HD), 1) < HD // 2, -1.0, 1.0)
    return cb * cf - sb * sf, sign * (sb * cf + cb * sf)


def rotate(x, cos, sin):
    return x * cos + pltpu.roll(x, HD // 2, 1) * sin


DX = (0, -1, 1, 2)
DZ = (0, -1, 1, -2, 2, -3, 3, 4)
Q_AT, O_AT, KV_AT, POS = 0, 64, 128, 160


def piece_tables(x, z, c, y):
    cc = jnp.stack([c, 1 - c])[:, None, None]
    four, eight = np.array(DX), np.array(DZ)

    def group(dx, dz):
        zs = (z + dz) & 7
        return (((x + dx) & 3) * 4 + (zs & 3)) * 2 + cc, zs >> 2

    gq, hq = group(four[None, None, :], eight[None, :, None])
    go, ho = group(four[None, :, None], eight[None, None, :])
    gk, _ = group(four[None, :, None], four[None, None, :])
    parts = (gq * 2 + hq, go * 2 + ho, gk)
    parts += (y, z >> 2)
    return jnp.concatenate([t.reshape(-1) for t in parts]).astype(jnp.int32)


def fetch(tab, base, refs, w, sem):
    for ref in refs:

        def start(j, carry, ref=ref, base=base):
            at = tab[base + j]
            cols = pl.ds(pl.multiple_of((at & 1) * (2 * HD), 2 * HD), 2 * HD)
            pltpu.make_async_copy(ref.at[j], w.at[:, at >> 1, :, cols], sem).start()
            return carry

        lax.fori_loop(0, ref.shape[0], start, 0)
        base += ref.shape[0]


def attend(i, zh, mask, q, k, v, s, out):
    b = 2 * i + zh
    diff = lax.broadcasted_iota(jnp.int32, (BLK, BLK), 1) - lax.broadcasted_iota(
        jnp.int32, (BLK, BLK), 0
    )
    diff = jnp.concatenate([diff, diff], axis=0)

    def heads(n, carry):
        qq = q[i, pl.ds(pl.multiple_of(n * 2 * BLK, 2 * BLK), 2 * BLK), :]
        for j in range(NBLK):
            mb = mask[b, j]
            off = jnp.where(mb == 1, 4096, jnp.where(mb == 2, BLK * (b - j), -4096))
            sj = lax.dot_general(
                qq,
                k[j * BLK : (j + 1) * BLK, :],
                (((1,), (1,)), ((), ())),
                preferred_element_type=jnp.float32,
            )
            s[:, j * BLK : (j + 1) * BLK] = jnp.where(diff <= off, sj, NEG)
        sv = s[...]
        p = jnp.exp((sv - jnp.max(sv, axis=1, keepdims=True)) * (HD**-0.5))
        total = jnp.sum(p, axis=1, keepdims=True)
        a = jnp.dot(p.astype(BF), v[...], preferred_element_type=jnp.float32) / total
        a = a.astype(BF)
        cols = pl.ds(pl.multiple_of(n * 2 * HD, 2 * HD), 2 * HD)
        out[:, cols] = jnp.concatenate([a[:BLK], a[BLK:]], axis=1)
        return carry

    lax.fori_loop(0, HEADS // 2, heads, 0)


def project_out(a, w, sec, out, first, count):
    quarter = D // 4

    def chunk(g, carry):
        wt = w[sec, pl.ds(pl.multiple_of(8 * (first + g), 8), 8)].reshape(quarter, WID)
        r = lax.dot_general(a, wt, (((1,), (1,)), ((), ())), preferred_element_type=jnp.float32)
        out[:, pl.ds(pl.multiple_of(g * quarter, BLK), quarter)] = r.astype(BF)
        return carry

    lax.fori_loop(0, count, chunk, 0)


def head_body(mod, mask, tab, *refs):
    kv_refs, q_refs, o_refs, x_hbm, tables = refs[:6], refs[6:17], refs[17:24], refs[24], refs[25:29]
    q, k, v = refs[29:32]
    outs = refs[32:34]
    x, wk, wq, wo, att, s, inv, xsem, ksem, qsem, osem = refs[34:]
    y0, zh = tab[POS], tab[POS + 1]
    for a in range(4):

        def start(j, carry, a=a):
            at = [tab[KV_AT + n * 16 + a * 4 + j] for n in range(2)]
            if a < 3:
                pltpu.make_async_copy(kv_refs[a].at[:, j], wk.at[:, at[0]], ksem).start()
            else:
                for m in range(2):
                    pltpu.make_async_copy(kv_refs[3 + m].at[j], wk.at[m, at[0]], ksem).start()
            src = kv_refs[5].at[pl.ds(2 * a, 2), j]
            pltpu.make_async_copy(src, wk.at[:, at[1]], ksem).start()
            return carry

        lax.fori_loop(0, 4, start, 0)
    order = [2 * i + zh for i in range(QB)] + [2 * i + 1 - zh for i in range(QB)]
    kinds = [mod[b] for b in order]
    n1 = sum(kinds)
    h0 = (NBLK - n1 + 1) // 2
    passes = h0 + (n1 + 1) // 2
    for t in range(NBLK + 2):
        inv[t] = -1
    c0, c1 = 0, 0
    for n, (b, kind) in enumerate(zip(order, kinds)):
        inv[jnp.where(kind == 0, c0, 2 * h0 + c1)] = b
        c0, c1 = c0 + 1 - kind, c1 + kind
        if n == QB - 1:
            p0, p1 = (c0 + 1) // 2, (c1 + 1) // 2

    def block_copy(t):
        rows = pl.ds(pl.multiple_of(inv[t] * BLK, BLK), BLK)
        return pltpu.make_async_copy(x_hbm.at[rows], x.at[t], xsem.at[t])

    def start_x(t, carry):
        @pl.when(inv[t] >= 0)
        def _():
            block_copy(t).start()

        return carry

    lax.fori_loop(0, NBLK + 2, start_x, 0)
    fetch(tab, Q_AT, q_refs, wq, qsem)
    fetch(tab, O_AT, o_refs, wo, osem)
    pltpu.make_async_copy(wk, wk, ksem).wait()

    def project_kv(p, carry):
        sec = jnp.where(p >= h0, 1, 0)
        ids = [inv[2 * p + t] for t in range(2)]
        for t in range(2):

            @pl.when(ids[t] >= 0)
            def _():
                block_copy(2 * p + t).wait()

        lhs = x[pl.ds(2 * p, 2)].reshape(2 * BLK, D)
        y = jnp.dot(lhs, wk[sec].reshape(D, 2 * HD), preferred_element_type=jnp.float32)
        for t in range(2):

            @pl.when(ids[t] >= 0)
            def _():
                yt = y[t * BLK : (t + 1) * BLK]
                cos, sin = block_tables(tables, ids[t])
                rows = pl.ds(pl.multiple_of(ids[t] * BLK, BLK), BLK)
                k[rows, :] = rotate(yt[:, :HD], cos, sin).astype(BF)
                v[rows, :] = yt[:, HD:].astype(BF)

        return carry

    lax.fori_loop(0, passes, project_kv, 0)
    pltpu.make_async_copy(wq, wq, qsem).wait()

    def project_q(p, carry):
        sec = jnp.where(p >= p0, 1, 0)
        slot = jnp.where(p >= p0, 2 * (h0 + p - p0), 2 * p)
        lhs = x[pl.ds(slot, 2)].reshape(2 * BLK, D)
        y = jnp.dot(lhs, wq[sec].reshape(D, WID), preferred_element_type=jnp.float32)
        for t in range(2):
            b = inv[slot + t]

            @pl.when((b >= 0) & ((b & 1) == zh))
            def _():
                cos, sin = block_tables(tables, b)
                for h in range(HEADS):
                    yt = y[t * BLK : (t + 1) * BLK, h * HD : (h + 1) * HD]
                    q[b >> 1, h * BLK : (h + 1) * BLK, :] = rotate(yt, cos, sin).astype(BF)

        return carry

    lax.fori_loop(0, p0 + p1, project_q, 0)
    far = (y0 + 2) & 3
    attend(far, zh, mask, q, k, v, s, att)
    pltpu.make_async_copy(wo, wo, osem).wait()
    for n in range(2):
        project_out(att[...], wo, mod[2 * far + zh], outs[n], 2 * n, 2)


def tail_body(first, count, mod, mask, tab, *refs):
    o_refs, (q, k, v), outs, (wo, att, s, osem) = refs[:7], refs[7:10], refs[10:-4], refs[-4:]
    y0, zh = tab[POS], tab[POS + 1]
    fetch(tab, O_AT, o_refs, wo, osem)

    def one(n, carry):
        attend((y0 + first + 2 * n) & 3, zh, mask, q, k, v, s, att.at[n])
        return carry

    lax.fori_loop(0, count, one, 0)
    pltpu.make_async_copy(wo, wo, osem).wait()

    for n, out in enumerate(outs):
        sec = mod[2 * ((y0 + first + 2 * n) & 3) + zh]
        project_out(att[n], wo, sec, out, 0, 4)


VM = pl.BlockSpec(memory_space=pltpu.VMEM)
BF = jnp.bfloat16
HALF_BLOCK = jax.ShapeDtypeStruct((BLK, D // 2), BF)


def head(mod, mask, tab, kv_all, q_all, o_all, x, tables):
    return pl.pallas_call(
        head_body,
        out_shape=[
            jax.ShapeDtypeStruct((QB, HEADS * BLK, HD), BF),
            jax.ShapeDtypeStruct((SEQ, HD), BF),
            jax.ShapeDtypeStruct((SEQ, HD), BF),
            HALF_BLOCK,
            HALF_BLOCK,
        ],
        in_specs=[SM] * 3 + [ANY] * 25 + [VM] * 4,
        out_specs=[VM] * 5,
        scratch_shapes=[
            pltpu.VMEM((NBLK + 2, BLK, D), BF),
            pltpu.VMEM((2, NG, ROWS, 2 * HD), BF),
            pltpu.VMEM((2, NG, ROWS, WID), BF),
            pltpu.VMEM((2, NG, ROWS, WID), BF),
            pltpu.VMEM((BLK, WID), BF),
            pltpu.VMEM((2 * BLK, SEQ), jnp.float32),
            pltpu.SMEM((NBLK + 2,), jnp.int32),
            pltpu.SemaphoreType.DMA((NBLK + 2,)),
            pltpu.SemaphoreType.DMA,
            pltpu.SemaphoreType.DMA,
            pltpu.SemaphoreType.DMA,
        ],
        name="head",
        cost_estimate=pl.CostEstimate(
            flops=2 * SEQ * D * 2 * HD + 2 * QB * BLK * D * WID,
            bytes_accessed=2 * SEQ * D + 8 * D * HD + 8 * D * WID,
            transcendentals=BLK * HEADS * SEQ,
        ),
    )(mod, mask, tab, *kv_all, *q_all, *o_all, x, *tables)


def tail(first, count, mod, mask, tab, o_all, q, k, v):
    return pl.pallas_call(
        functools.partial(tail_body, first, count),
        out_shape=[jax.ShapeDtypeStruct((BLK, D), BF)] * count,
        in_specs=[SM] * 3 + [ANY] * 7 + [VM] * 3,
        out_specs=[VM] * count,
        scratch_shapes=[
            pltpu.VMEM((2, NG, ROWS, WID), BF),
            pltpu.VMEM((count, BLK, WID), BF),
            pltpu.VMEM((2 * BLK, SEQ), jnp.float32),
            pltpu.SemaphoreType.DMA,
        ],
        name="tail",
        cost_estimate=pl.CostEstimate(
            flops=count * (2 * BLK * D * WID + 4 * BLK * SEQ * WID),
            bytes_accessed=4 * D * WID,
            transcendentals=count * BLK * HEADS * SEQ,
        ),
    )(mod, mask, tab, *o_all, q, k, v)


def along_x(a, step):
    return lax.ppermute(a, "x", [(i, (i + step) % 4) for i in range(4)])


def along_z(a, step):
    at = [(z & 3) * 2 + (z >> 2) for z in range(8)]
    return lax.ppermute(a, ("zl", "zh"), [(at[z], at[(z + step) % 8]) for z in range(8)])


def swap(a):
    return lax.ppermute(a, "c", [(0, 1), (1, 0)])


def gather(kv, q, o, at):
    p1p, p1m = along_x(q, 1), along_x(q, -1)
    own = jnp.concatenate([kv[:1], o, kv[1:]], axis=0)
    r1p, r1m = along_z(own, 1), along_z(own, -1)
    p2p, p2m = along_x(p1p[0], 1), along_x(p1m[1], -1)
    r2p, r2m = along_z(r1p[:3], 1), along_z(r1m[1:], -1)
    kb = jnp.stack(
        [
            jnp.stack([own[0], r1p[0], r1m[0], r2p[0]]),
            jnp.stack([own[3], r1p[3], r1m[3], r2m[2]]),
        ]
    )
    k1p, k1m = along_x(kb, 1), along_x(kb, -1)
    r2p, r2m = r2p[1:], r2m[:2]
    r3p, r3m = along_z(r2p, 1), along_z(r2m, -1)
    b = jnp.stack([q, p1p, p1m, jnp.stack([p2p, p2m])])
    b, r3p, r3m = lax.optimization_barrier((b, r3p, r3m))
    r4 = jnp.stack([along_z(r3p[0], 1), along_z(r3m[1], -1)])
    t1p, t1m = along_z(b, 1), along_z(b, -1)
    t1p, t1m, _, k1p, k1m = lax.optimization_barrier((t1p, t1m, r4, k1p, k1m))
    ob = jnp.stack([o, r1p[1:3], r1m[1:3], r2p, r2m, r3p, r3m, r4])
    o1p, o1m = along_x(ob, 1), along_x(ob, -1)
    t2p, t2m = along_z(t1p, 1), along_z(t1m, -1)
    k2p, k2m = along_x(k1p[0], 1), along_x(k1m[1], -1)
    kv_all = [kb, k1p, k1m, k2p, k2m]
    kv_all.append(swap(jnp.concatenate([kb, k1p, k1m, jnp.stack([k2p, k2m])])))
    t2p, t2m, at = lax.optimization_barrier((t2p, t2m, at))
    tab = piece_tables(*at)
    t3p, t3m = along_z(t2p, 1), along_z(t2m, -1)
    o2p, o2m = along_x(o1p[:4], 1), along_x(o1m[4:], -1)
    t4p, t4m = along_z(t3p[:2], 1), along_z(t3m[2:], -1)
    q_all = [b, t1p, t1m, t2p, t2m, t3p, t3m, t4p, t4m]
    q_all.append(swap(jnp.concatenate([b, t1p, t1m, t2p, t2m])))
    q_all.append(swap(jnp.concatenate([t3p, t3m, t4p, t4m])))
    o_all = [ob, o1p, o1m, o2p, o2m]
    o_all.append(swap(jnp.concatenate([ob, o1p, o1m])))
    o_all.append(swap(jnp.concatenate([o2p, o2m])))
    return kv_all, q_all, o_all, tab


def local(tokens, modality, block_mask, q_weight, kv_weight, o_weight):
    y, zh, c = lax.axis_index("y"), lax.axis_index("zh"), lax.axis_index("c")
    at = (lax.axis_index("x"), zh * 4 + lax.axis_index("zl"), c, y)
    tables = [jnp.asarray(t) for t in rotary_tables()]
    kv = lax.dynamic_slice_in_dim(kv_weight, y * (2 * HD), 2 * HD, 2)
    kv_all, q_all, o_all, tab = gather(kv, q_weight, jnp.swapaxes(o_weight, 1, 2), at)
    small = (modality[0], block_mask[0], tab)
    q, k, v, o2a, o2b = head(*small, kv_all, q_all, o_all, tokens[0], tables)
    up = [(i, (i + 1) % NY) for i in range(NY)]
    down = [(i, (i - 1) % NY) for i in range(NY)]
    f32, half = jnp.float32, D // 2

    def add(a, b):
        return (a.astype(f32) + b.astype(f32)).astype(BF)

    far_a = lax.ppermute(o2a, "y", up)
    far_b = lax.ppermute(o2b, "y", down)
    o3, o1 = tail(3, 2, *small, o_all, q, k, v)
    p = jnp.concatenate([add(o1[:, :half], far_a), o1[:, half:]], axis=1)
    m = jnp.concatenate([o3[:, :half], add(o3[:, half:], far_b)], axis=1)
    p = lax.ppermute(p, "y", up)
    m = lax.ppermute(m, "y", down)
    o0 = tail(0, 1, *small, o_all, q, k, v)[0]
    return (o0.astype(f32) + p.astype(f32) + m.astype(f32)).astype(BF)[None]


def solution(mesh):
    fine = Mesh(mesh.devices.reshape(4, 4, 2, 4, 2), ("x", "zl", "c", "y", "zh"))
    dp = ("x", "zl", "c")
    mp = ("y", "zh")
    in_specs = (
        P(dp, None, None),
        P(dp, None),
        P(dp, None, None),
        P(None, dp, mp),
        P(None, dp, None),
        P(None, mp, dp),
    )
    return jax.shard_map(local, mesh=fine, in_specs=in_specs, out_specs=P(dp, mp, None), check_vma=False)
```

```python
import functools

import jax
import jax.numpy as jnp
import numpy as np
from jax import lax
from jax.experimental import pallas as pl
from jax.experimental.pallas import tpu as pltpu
from jax.sharding import Mesh
from jax.sharding import PartitionSpec as P

D = 3584
HD = 128
BLK = 128
NBLK = 8
SEQ = 1024
ROWS = 112
NG = 32
NY = 4
QB = 4
HEADS = 4
WID = HEADS * HD
ROPE_THETA = 1000000.0
NEG = -1e30
ANY = pl.BlockSpec(memory_space=pl.ANY)
SM = pl.BlockSpec(memory_space=pltpu.SMEM)


def rotary_tables():
    half = HD // 2
    freq = ROPE_THETA ** (-np.arange(half, dtype=np.float64) * 2.0 / HD)
    freq = np.concatenate([freq, freq])[None, :]
    fine = np.arange(BLK, dtype=np.float64)[:, None] * freq
    base = BLK * np.arange(NBLK, dtype=np.float64)[:, None] * freq
    return [np.asarray(t, np.float32) for t in (np.cos(fine), np.sin(fine), np.cos(base), np.sin(base))]


def block_tables(tables, b):
    cf, sf = tables[0][...], tables[1][...]
    cb, sb = tables[2][pl.ds(b, 1), :], tables[3][pl.ds(b, 1), :]
    sign = jnp.where(lax.broadcasted_iota(jnp.int32, (1, HD), 1) < HD // 2, -1.0, 1.0)
    return cb * cf - sb * sf, sign * (sb * cf + cb * sf)


def rotate(x, cos, sin):
    return x * cos + pltpu.roll(x, HD // 2, 1) * sin


DX = (0, -1, 1, 2)
DZ = (0, -1, 1, -2, 2, -3, 3, 4)
Q_AT, O_AT, KV_AT, POS = 0, 64, 128, 160


def piece_tables(x, z, c, y):
    cc = jnp.stack([c, 1 - c])[:, None, None]
    four, eight = np.array(DX), np.array(DZ)

    def group(dx, dz):
        zs = (z + dz) & 7
        return (((x + dx) & 3) * 4 + (zs & 3)) * 2 + cc, zs >> 2

    gq, hq = group(four[None, None, :], eight[None, :, None])
    go, ho = group(four[None, :, None], eight[None, None, :])
    gk, _ = group(four[None, :, None], four[None, None, :])
    parts = (gq * 2 + hq, go * 2 + ho, gk)
    parts += (y, z >> 2)
    return jnp.concatenate([t.reshape(-1) for t in parts]).astype(jnp.int32)


def fetch(tab, base, refs, w, sem):
    for ref in refs:

        def start(j, carry, ref=ref, base=base):
            at = tab[base + j]
            cols = pl.ds(pl.multiple_of((at & 1) * (2 * HD), 2 * HD), 2 * HD)
            pltpu.make_async_copy(ref.at[j], w.at[:, at >> 1, :, cols], sem).start()
            return carry

        lax.fori_loop(0, ref.shape[0], start, 0)
        base += ref.shape[0]


def attend(i, zh, mask, q, k, v, s, out):
    b = 2 * i + zh
    diff = lax.broadcasted_iota(jnp.int32, (BLK, BLK), 1) - lax.broadcasted_iota(
        jnp.int32, (BLK, BLK), 0
    )
    diff = jnp.concatenate([diff, diff], axis=0)

    def heads(n, carry):
        qq = q[i, pl.ds(pl.multiple_of(n * 2 * BLK, 2 * BLK), 2 * BLK), :]
        for j in range(NBLK):
            mb = mask[b, j]
            off = jnp.where(mb == 1, 4096, jnp.where(mb == 2, BLK * (b - j), -4096))
            sj = lax.dot_general(
                qq,
                k[j * BLK : (j + 1) * BLK, :],
                (((1,), (1,)), ((), ())),
                preferred_element_type=jnp.float32,
            )
            s[:, j * BLK : (j + 1) * BLK] = jnp.where(diff <= off, sj, NEG)
        sv = s[...]
        p = jnp.exp((sv - jnp.max(sv, axis=1, keepdims=True)) * (HD**-0.5))
        total = jnp.sum(p, axis=1, keepdims=True)
        a = jnp.dot(p.astype(BF), v[...], preferred_element_type=jnp.float32) / total
        a = a.astype(BF)
        cols = pl.ds(pl.multiple_of(n * 2 * HD, 2 * HD), 2 * HD)
        out[:, cols] = jnp.concatenate([a[:BLK], a[BLK:]], axis=1)
        return carry

    lax.fori_loop(0, HEADS // 2, heads, 0)


def project_out(a, w, sec, out, first, count):
    quarter = D // 4

    def chunk(g, carry):
        wt = w[sec, pl.ds(pl.multiple_of(8 * (first + g), 8), 8)].reshape(quarter, WID)
        r = lax.dot_general(a, wt, (((1,), (1,)), ((), ())), preferred_element_type=jnp.float32)
        out[:, pl.ds(pl.multiple_of(g * quarter, BLK), quarter)] = r.astype(BF)
        return carry

    lax.fori_loop(0, count, chunk, 0)


def head_body(mod, mask, tab, *refs):
    kv_refs, q_refs, o_refs, x_hbm, tables = refs[:6], refs[6:18], refs[18:25], refs[25], refs[26:30]
    q, k, v = refs[30:33]
    outs = refs[33:35]
    x, wk, wq, wo, att, s, inv, xsem, ksem, qsem, osem = refs[35:]
    y0, zh = tab[POS], tab[POS + 1]
    for a in range(4):

        def start(j, carry, a=a):
            at = [tab[KV_AT + n * 16 + a * 4 + j] for n in range(2)]
            if a < 3:
                pltpu.make_async_copy(kv_refs[a].at[:, j], wk.at[:, at[0]], ksem).start()
            else:
                for m in range(2):
                    pltpu.make_async_copy(kv_refs[3 + m].at[j], wk.at[m, at[0]], ksem).start()
            src = kv_refs[5].at[pl.ds(2 * a, 2), j]
            pltpu.make_async_copy(src, wk.at[:, at[1]], ksem).start()
            return carry

        lax.fori_loop(0, 4, start, 0)
    order = [2 * i + zh for i in range(QB)] + [2 * i + 1 - zh for i in range(QB)]
    kinds = [mod[b] for b in order]
    n1 = sum(kinds)
    h0 = (NBLK - n1 + 1) // 2
    passes = h0 + (n1 + 1) // 2
    for t in range(NBLK + 2):
        inv[t] = -1
    c0, c1 = 0, 0
    for n, (b, kind) in enumerate(zip(order, kinds)):
        inv[jnp.where(kind == 0, c0, 2 * h0 + c1)] = b
        c0, c1 = c0 + 1 - kind, c1 + kind
        if n == QB - 1:
            p0, p1 = (c0 + 1) // 2, (c1 + 1) // 2

    def block_copy(t):
        rows = pl.ds(pl.multiple_of(inv[t] * BLK, BLK), BLK)
        return pltpu.make_async_copy(x_hbm.at[rows], x.at[t], xsem.at[t])

    def start_x(t, carry):
        @pl.when(inv[t] >= 0)
        def _():
            block_copy(t).start()

        return carry

    lax.fori_loop(0, NBLK + 2, start_x, 0)
    fetch(tab, Q_AT, q_refs, wq, qsem)
    fetch(tab, O_AT, o_refs, wo, osem)
    pltpu.make_async_copy(wk, wk, ksem).wait()

    def project_kv(p, carry):
        sec = jnp.where(p >= h0, 1, 0)
        ids = [inv[2 * p + t] for t in range(2)]
        for t in range(2):

            @pl.when(ids[t] >= 0)
            def _():
                block_copy(2 * p + t).wait()

        lhs = x[pl.ds(2 * p, 2)].reshape(2 * BLK, D)
        y = jnp.dot(lhs, wk[sec].reshape(D, 2 * HD), preferred_element_type=jnp.float32)
        for t in range(2):

            @pl.when(ids[t] >= 0)
            def _():
                yt = y[t * BLK : (t + 1) * BLK]
                cos, sin = block_tables(tables, ids[t])
                rows = pl.ds(pl.multiple_of(ids[t] * BLK, BLK), BLK)
                k[rows, :] = rotate(yt[:, :HD], cos, sin).astype(BF)
                v[rows, :] = yt[:, HD:].astype(BF)

        return carry

    lax.fori_loop(0, passes, project_kv, 0)
    pltpu.make_async_copy(wq, wq, qsem).wait()

    def project_q(p, carry):
        sec = jnp.where(p >= p0, 1, 0)
        slot = jnp.where(p >= p0, 2 * (h0 + p - p0), 2 * p)
        lhs = x[pl.ds(slot, 2)].reshape(2 * BLK, D)
        y = jnp.dot(lhs, wq[sec].reshape(D, WID), preferred_element_type=jnp.float32)
        for t in range(2):
            b = inv[slot + t]

            @pl.when((b >= 0) & ((b & 1) == zh))
            def _():
                cos, sin = block_tables(tables, b)
                for h in range(HEADS):
                    yt = y[t * BLK : (t + 1) * BLK, h * HD : (h + 1) * HD]
                    q[b >> 1, h * BLK : (h + 1) * BLK, :] = rotate(yt, cos, sin).astype(BF)

        return carry

    lax.fori_loop(0, p0 + p1, project_q, 0)
    far = (y0 + 2) & 3
    attend(far, zh, mask, q, k, v, s, att)
    pltpu.make_async_copy(wo, wo, osem).wait()
    for n in range(2):
        project_out(att[...], wo, mod[2 * far + zh], outs[n], 2 * n, 2)


def tail_body(first, count, mod, mask, tab, *refs):
    o_refs, (q, k, v), outs, (wo, att, s, osem) = refs[:7], refs[7:10], refs[10:-4], refs[-4:]
    y0, zh = tab[POS], tab[POS + 1]
    fetch(tab, O_AT, o_refs, wo, osem)

    def one(n, carry):
        attend((y0 + first + 2 * n) & 3, zh, mask, q, k, v, s, att.at[n])
        return carry

    lax.fori_loop(0, count, one, 0)
    pltpu.make_async_copy(wo, wo, osem).wait()

    for n, out in enumerate(outs):
        sec = mod[2 * ((y0 + first + 2 * n) & 3) + zh]
        project_out(att[n], wo, sec, out, 0, 4)


VM = pl.BlockSpec(memory_space=pltpu.VMEM)
BF = jnp.bfloat16
HALF_BLOCK = jax.ShapeDtypeStruct((BLK, D // 2), BF)


def head(mod, mask, tab, kv_all, q_all, o_all, x, tables):
    return pl.pallas_call(
        head_body,
        out_shape=[
            jax.ShapeDtypeStruct((QB, HEADS * BLK, HD), BF),
            jax.ShapeDtypeStruct((SEQ, HD), BF),
            jax.ShapeDtypeStruct((SEQ, HD), BF),
            HALF_BLOCK,
            HALF_BLOCK,
        ],
        in_specs=[SM] * 3 + [ANY] * 26 + [VM] * 4,
        out_specs=[VM] * 5,
        scratch_shapes=[
            pltpu.VMEM((NBLK + 2, BLK, D), BF),
            pltpu.VMEM((2, NG, ROWS, 2 * HD), BF),
            pltpu.VMEM((2, NG, ROWS, WID), BF),
            pltpu.VMEM((2, NG, ROWS, WID), BF),
            pltpu.VMEM((BLK, WID), BF),
            pltpu.VMEM((2 * BLK, SEQ), jnp.float32),
            pltpu.SMEM((NBLK + 2,), jnp.int32),
            pltpu.SemaphoreType.DMA((NBLK + 2,)),
            pltpu.SemaphoreType.DMA,
            pltpu.SemaphoreType.DMA,
            pltpu.SemaphoreType.DMA,
        ],
        name="head",
        cost_estimate=pl.CostEstimate(
            flops=2 * SEQ * D * 2 * HD + 2 * QB * BLK * D * WID,
            bytes_accessed=2 * SEQ * D + 8 * D * HD + 8 * D * WID,
            transcendentals=BLK * HEADS * SEQ,
        ),
    )(mod, mask, tab, *kv_all, *q_all, *o_all, x, *tables)


def tail(first, count, mod, mask, tab, o_all, q, k, v):
    return pl.pallas_call(
        functools.partial(tail_body, first, count),
        out_shape=[jax.ShapeDtypeStruct((BLK, D), BF)] * count,
        in_specs=[SM] * 3 + [ANY] * 7 + [VM] * 3,
        out_specs=[VM] * count,
        scratch_shapes=[
            pltpu.VMEM((2, NG, ROWS, WID), BF),
            pltpu.VMEM((count, BLK, WID), BF),
            pltpu.VMEM((2 * BLK, SEQ), jnp.float32),
            pltpu.SemaphoreType.DMA,
        ],
        name="tail",
        cost_estimate=pl.CostEstimate(
            flops=count * (2 * BLK * D * WID + 4 * BLK * SEQ * WID),
            bytes_accessed=4 * D * WID,
            transcendentals=count * BLK * HEADS * SEQ,
        ),
    )(mod, mask, tab, *o_all, q, k, v)


def along_x(a, step):
    return lax.ppermute(a, "x", [(i, (i + step) % 4) for i in range(4)])


def along_z(a, step):
    at = [(z & 3) * 2 + (z >> 2) for z in range(8)]
    return lax.ppermute(a, ("zl", "zh"), [(at[z], at[(z + step) % 8]) for z in range(8)])


def swap(a):
    return lax.ppermute(a, "c", [(0, 1), (1, 0)])


def gather(kv, q, o, at):
    p1p, p1m = along_x(q, 1), along_x(q, -1)
    own = jnp.concatenate([kv[:1], o, kv[1:]], axis=0)
    r1p, r1m = along_z(own, 1), along_z(own, -1)
    p2 = along_x(q, 2)
    r2p, r2m = along_z(r1p[:3], 1), along_z(r1m[1:], -1)
    kb = jnp.stack(
        [
            jnp.stack([own[0], r1p[0], r1m[0], r2p[0]]),
            jnp.stack([own[3], r1p[3], r1m[3], r2m[2]]),
        ]
    )
    k1p, k1m = along_x(kb, 1), along_x(kb, -1)
    r2p, r2m = r2p[1:], r2m[:2]
    r3p, r3m = along_z(r2p, 1), along_z(r2m, -1)
    b = jnp.stack([q, p1p, p1m, p2])
    b, r3p, r3m = lax.optimization_barrier((b, r3p, r3m))
    r4 = jnp.stack([along_z(r3p[0], 1), along_z(r3m[1], -1)])
    t1p, t1m = along_z(b, 1), along_z(b, -1)
    t1p, t1m, _, k1p, k1m = lax.optimization_barrier((t1p, t1m, r4, k1p, k1m))
    ob = jnp.stack([o, r1p[1:3], r1m[1:3], r2p, r2m, r3p, r3m, r4])
    o1p, o1m = along_x(ob, 1), along_x(ob, -1)
    t2p, t2m = along_z(t1p, 1), along_z(t1m, -1)
    k2p, k2m = along_x(k1p[0], 1), along_x(k1m[1], -1)
    t2p, t2m, at = lax.optimization_barrier((t2p, t2m, at))
    tab = piece_tables(*at)
    t3p, t3m = along_z(t2p, 1), along_z(t2m, -1)
    k2p, k2m = lax.optimization_barrier((k2p, k2m, t3p, t3m))[:2]
    kv_all = [kb, k1p, k1m, k2p, k2m]
    kv_all.append(swap(jnp.concatenate([kb, k1p, k1m, jnp.stack([k2p, k2m])])))
    o2p, o2m = along_x(o1p[:4], 1), along_x(o1m[4:], -1)
    t4p, t4m = along_z(t3p[:2], 1), along_z(t3m[2:], -1)
    q_all = [b, t1p, t1m, t2p, t2m, t3p, t3m, t4p, t4m]
    q_all.append(swap(jnp.concatenate([b, t1p, t1m, t2p, t2m])))
    q_all.append(swap(jnp.concatenate([t3p, t3m])))
    q_all.append(swap(jnp.concatenate([t4p, t4m])))
    o_all = [ob, o1p, o1m, o2p, o2m]
    o_all.append(swap(jnp.concatenate([ob, o1p, o1m])))
    o_all.append(swap(jnp.concatenate([o2p, o2m])))
    return kv_all, q_all, o_all, tab


def local(tokens, modality, block_mask, q_weight, kv_weight, o_weight):
    y, zh, c = lax.axis_index("y"), lax.axis_index("zh"), lax.axis_index("c")
    at = (lax.axis_index("x"), zh * 4 + lax.axis_index("zl"), c, y)
    tables = [jnp.asarray(t) for t in rotary_tables()]
    kv = lax.dynamic_slice_in_dim(kv_weight, y * (2 * HD), 2 * HD, 2)
    kv_all, q_all, o_all, tab = gather(kv, q_weight, jnp.swapaxes(o_weight, 1, 2), at)
    small = (modality[0], block_mask[0], tab)
    q, k, v, o2a, o2b = head(*small, kv_all, q_all, o_all, tokens[0], tables)
    up = [(i, (i + 1) % NY) for i in range(NY)]
    down = [(i, (i - 1) % NY) for i in range(NY)]
    f32, half = jnp.float32, D // 2

    def add(a, b):
        return (a.astype(f32) + b.astype(f32)).astype(BF)

    far_a = lax.ppermute(o2a, "y", up)
    far_b = lax.ppermute(o2b, "y", down)
    o3, o1 = tail(3, 2, *small, o_all, q, k, v)
    p = lax.dynamic_update_slice(o1, add(o1[:, :half], far_a), (0, 0))
    m = lax.dynamic_update_slice(o3, add(o3[:, half:], far_b), (0, half))
    p = lax.ppermute(p, "y", up)
    m = lax.ppermute(m, "y", down)
    o0 = tail(0, 1, *small, o_all, q, k, v)[0]
    return (o0.astype(f32) + p.astype(f32) + m.astype(f32)).astype(BF)[None]


def solution(mesh):
    fine = Mesh(mesh.devices.reshape(4, 4, 2, 4, 2), ("x", "zl", "c", "y", "zh"))
    dp = ("x", "zl", "c")
    mp = ("y", "zh")
    in_specs = (
        P(dp, None, None),
        P(dp, None),
        P(dp, None, None),
        P(None, dp, mp),
        P(None, dp, None),
        P(None, mp, dp),
    )
    return jax.shard_map(
        local, mesh=fine, in_specs=in_specs, out_specs=P(dp, mp, None), check_vma=False
    )
```

```python
import functools

import jax
import jax.numpy as jnp
import numpy as np
from jax import lax
from jax.experimental import pallas as pl
from jax.experimental.pallas import tpu as pltpu
from jax.sharding import Mesh
from jax.sharding import PartitionSpec as P

D = 3584
HD = 128
BLK = 128
NBLK = 8
SEQ = 1024
ROWS = 112
NG = 32
NY = 4
QB = 4
HEADS = 4
WID = HEADS * HD
ROPE_THETA = 1000000.0
NEG = -1e30
ANY = pl.BlockSpec(memory_space=pl.ANY)
SM = pl.BlockSpec(memory_space=pltpu.SMEM)


def rotary_tables():
    half = HD // 2
    freq = ROPE_THETA ** (-np.arange(half, dtype=np.float64) * 2.0 / HD)
    freq = np.concatenate([freq, freq])[None, :]
    fine = np.arange(BLK, dtype=np.float64)[:, None] * freq
    base = BLK * np.arange(NBLK, dtype=np.float64)[:, None] * freq
    return [np.asarray(t, np.float32) for t in (np.cos(fine), np.sin(fine), np.cos(base), np.sin(base))]


def block_tables(tables, b):
    cf, sf = tables[0][...], tables[1][...]
    cb, sb = tables[2][pl.ds(b, 1), :], tables[3][pl.ds(b, 1), :]
    sign = jnp.where(lax.broadcasted_iota(jnp.int32, (1, HD), 1) < HD // 2, -1.0, 1.0)
    return cb * cf - sb * sf, sign * (sb * cf + cb * sf)


def rotate(x, cos, sin):
    return x * cos + pltpu.roll(x, HD // 2, 1) * sin


DX = (0, -1, 1, 2)
DZ = (0, -1, 1, -2, 2, -3, 3, 4)
Q_AT, O_AT, KV_AT, POS = 0, 64, 128, 160


def piece_tables(x, z, c, y):
    cc = jnp.stack([c, 1 - c])[:, None, None]
    four, eight = np.array(DX), np.array(DZ)

    def group(dx, dz):
        zs = (z + dz) & 7
        return (((x + dx) & 3) * 4 + (zs & 3)) * 2 + cc, zs >> 2

    gq, hq = group(four[None, None, :], eight[None, :, None])
    go, ho = group(four[None, :, None], eight[None, None, :])
    gk, _ = group(four[None, :, None], four[None, None, :])
    parts = (gq * 2 + hq, go * 2 + ho, gk)
    parts += (y, z >> 2)
    return jnp.concatenate([t.reshape(-1) for t in parts]).astype(jnp.int32)


def fetch(tab, base, refs, w, sem):
    for ref in refs:

        def start(j, carry, ref=ref, base=base):
            at = tab[base + j]
            cols = pl.ds(pl.multiple_of((at & 1) * (2 * HD), 2 * HD), 2 * HD)
            pltpu.make_async_copy(ref.at[j], w.at[:, at >> 1, :, cols], sem).start()
            return carry

        lax.fori_loop(0, ref.shape[0], start, 0)
        base += ref.shape[0]


def attend(i, zh, mask, q, k, v, s, out):
    b = 2 * i + zh
    diff = lax.broadcasted_iota(jnp.int32, (BLK, BLK), 1) - lax.broadcasted_iota(
        jnp.int32, (BLK, BLK), 0
    )
    diff = jnp.concatenate([diff, diff], axis=0)

    def heads(n, carry):
        qq = q[i, pl.ds(pl.multiple_of(n * 2 * BLK, 2 * BLK), 2 * BLK), :]
        for j in range(NBLK):
            mb = mask[b, j]
            off = jnp.where(mb == 1, 4096, jnp.where(mb == 2, BLK * (b - j), -4096))
            sj = lax.dot_general(
                qq,
                k[j * BLK : (j + 1) * BLK, :],
                (((1,), (1,)), ((), ())),
                preferred_element_type=jnp.float32,
            )
            s[:, j * BLK : (j + 1) * BLK] = jnp.where(diff <= off, sj, NEG)
        sv = s[...]
        p = jnp.exp((sv - jnp.max(sv, axis=1, keepdims=True)) * (HD**-0.5))
        total = jnp.sum(p, axis=1, keepdims=True)
        a = jnp.dot(p.astype(BF), v[...], preferred_element_type=jnp.float32) / total
        a = a.astype(BF)
        cols = pl.ds(pl.multiple_of(n * 2 * HD, 2 * HD), 2 * HD)
        out[:, cols] = jnp.concatenate([a[:BLK], a[BLK:]], axis=1)
        return carry

    lax.fori_loop(0, HEADS // 2, heads, 0)


def project_out(a, w, sec, out, first, count):
    quarter = D // 4

    def chunk(g, carry):
        wt = w[sec, pl.ds(pl.multiple_of(8 * (first + g), 8), 8)].reshape(quarter, WID)
        r = lax.dot_general(a, wt, (((1,), (1,)), ((), ())), preferred_element_type=jnp.float32)
        out[:, pl.ds(pl.multiple_of(g * quarter, BLK), quarter)] = r.astype(BF)
        return carry

    lax.fori_loop(0, count, chunk, 0)


def head_body(mod, mask, tab, *refs):
    kv_refs, q_refs, o_refs, x_hbm, tables = refs[:7], refs[7:20], refs[20:28], refs[28], refs[29:33]
    q, k, v = refs[33:36]
    outs = refs[36:38]
    x, wk, wq, wo, att, s, inv, xsem, ksem, qsem, osem = refs[38:]
    y0, zh = tab[POS], tab[POS + 1]
    for a in range(4):

        def start(j, carry, a=a):
            at = [tab[KV_AT + n * 16 + a * 4 + j] for n in range(2)]
            if a < 3:
                pltpu.make_async_copy(kv_refs[a].at[:, j], wk.at[:, at[0]], ksem).start()
            else:
                for m in range(2):
                    pltpu.make_async_copy(kv_refs[3 + m].at[j], wk.at[m, at[0]], ksem).start()
            src = kv_refs[5].at[pl.ds(2 * a, 2), j] if a < 3 else kv_refs[6].at[:, j]
            pltpu.make_async_copy(src, wk.at[:, at[1]], ksem).start()
            return carry

        lax.fori_loop(0, 4, start, 0)
    order = [2 * i + zh for i in range(QB)] + [2 * i + 1 - zh for i in range(QB)]
    kinds = [mod[b] for b in order]
    n1 = sum(kinds)
    h0 = (NBLK - n1 + 1) // 2
    passes = h0 + (n1 + 1) // 2
    for t in range(NBLK + 2):
        inv[t] = -1
    c0, c1 = 0, 0
    for n, (b, kind) in enumerate(zip(order, kinds)):
        inv[jnp.where(kind == 0, c0, 2 * h0 + c1)] = b
        c0, c1 = c0 + 1 - kind, c1 + kind
        if n == QB - 1:
            p0, p1 = (c0 + 1) // 2, (c1 + 1) // 2

    def block_copy(t):
        rows = pl.ds(pl.multiple_of(inv[t] * BLK, BLK), BLK)
        return pltpu.make_async_copy(x_hbm.at[rows], x.at[t], xsem.at[t])

    def start_x(t, carry):
        @pl.when(inv[t] >= 0)
        def _():
            block_copy(t).start()

        return carry

    lax.fori_loop(0, NBLK + 2, start_x, 0)
    fetch(tab, Q_AT, q_refs, wq, qsem)
    fetch(tab, O_AT, o_refs, wo, osem)
    pltpu.make_async_copy(wk, wk, ksem).wait()

    def project_kv(p, carry):
        sec = jnp.where(p >= h0, 1, 0)
        ids = [inv[2 * p + t] for t in range(2)]
        for t in range(2):

            @pl.when(ids[t] >= 0)
            def _():
                block_copy(2 * p + t).wait()

        lhs = x[pl.ds(2 * p, 2)].reshape(2 * BLK, D)
        y = jnp.dot(lhs, wk[sec].reshape(D, 2 * HD), preferred_element_type=jnp.float32)
        for t in range(2):

            @pl.when(ids[t] >= 0)
            def _():
                yt = y[t * BLK : (t + 1) * BLK]
                cos, sin = block_tables(tables, ids[t])
                rows = pl.ds(pl.multiple_of(ids[t] * BLK, BLK), BLK)
                k[rows, :] = rotate(yt[:, :HD], cos, sin).astype(BF)
                v[rows, :] = yt[:, HD:].astype(BF)

        return carry

    lax.fori_loop(0, passes, project_kv, 0)
    pltpu.make_async_copy(wq, wq, qsem).wait()

    def project_q(p, carry):
        sec = jnp.where(p >= p0, 1, 0)
        slot = jnp.where(p >= p0, 2 * (h0 + p - p0), 2 * p)
        lhs = x[pl.ds(slot, 2)].reshape(2 * BLK, D)
        y = jnp.dot(lhs, wq[sec].reshape(D, WID), preferred_element_type=jnp.float32)
        for t in range(2):
            b = inv[slot + t]

            @pl.when((b >= 0) & ((b & 1) == zh))
            def _():
                cos, sin = block_tables(tables, b)
                for h in range(HEADS):
                    yt = y[t * BLK : (t + 1) * BLK, h * HD : (h + 1) * HD]
                    q[b >> 1, h * BLK : (h + 1) * BLK, :] = rotate(yt, cos, sin).astype(BF)

        return carry

    lax.fori_loop(0, p0 + p1, project_q, 0)
    far = (y0 + 2) & 3
    attend(far, zh, mask, q, k, v, s, att)
    pltpu.make_async_copy(wo, wo, osem).wait()
    for n in range(2):
        project_out(att[...], wo, mod[2 * far + zh], outs[n], 2 * n, 2)


def tail_body(first, count, mod, mask, tab, *refs):
    o_refs, (q, k, v), outs, (wo, att, s, osem) = refs[:8], refs[8:11], refs[11:-4], refs[-4:]
    y0, zh = tab[POS], tab[POS + 1]
    fetch(tab, O_AT, o_refs, wo, osem)

    def one(n, carry):
        attend((y0 + first + 2 * n) & 3, zh, mask, q, k, v, s, att.at[n])
        return carry

    lax.fori_loop(0, count, one, 0)
    pltpu.make_async_copy(wo, wo, osem).wait()

    for n, out in enumerate(outs):
        sec = mod[2 * ((y0 + first + 2 * n) & 3) + zh]
        project_out(att[n], wo, sec, out, 0, 4)


VM = pl.BlockSpec(memory_space=pltpu.VMEM)
BF = jnp.bfloat16
HALF_BLOCK = jax.ShapeDtypeStruct((BLK, D // 2), BF)


def head(mod, mask, tab, kv_all, q_all, o_all, x, tables):
    return pl.pallas_call(
        head_body,
        out_shape=[
            jax.ShapeDtypeStruct((QB, HEADS * BLK, HD), BF),
            jax.ShapeDtypeStruct((SEQ, HD), BF),
            jax.ShapeDtypeStruct((SEQ, HD), BF),
            HALF_BLOCK,
            HALF_BLOCK,
        ],
        in_specs=[SM] * 3 + [ANY] * 29 + [VM] * 4,
        out_specs=[VM] * 5,
        scratch_shapes=[
            pltpu.VMEM((NBLK + 2, BLK, D), BF),
            pltpu.VMEM((2, NG, ROWS, 2 * HD), BF),
            pltpu.VMEM((2, NG, ROWS, WID), BF),
            pltpu.VMEM((2, NG, ROWS, WID), BF),
            pltpu.VMEM((BLK, WID), BF),
            pltpu.VMEM((2 * BLK, SEQ), jnp.float32),
            pltpu.SMEM((NBLK + 2,), jnp.int32),
            pltpu.SemaphoreType.DMA((NBLK + 2,)),
            pltpu.SemaphoreType.DMA,
            pltpu.SemaphoreType.DMA,
            pltpu.SemaphoreType.DMA,
        ],
        name="head",
        cost_estimate=pl.CostEstimate(
            flops=2 * SEQ * D * 2 * HD + 2 * QB * BLK * D * WID,
            bytes_accessed=2 * SEQ * D + 8 * D * HD + 8 * D * WID,
            transcendentals=BLK * HEADS * SEQ,
        ),
    )(mod, mask, tab, *kv_all, *q_all, *o_all, x, *tables)


def tail(first, count, mod, mask, tab, o_all, q, k, v):
    return pl.pallas_call(
        functools.partial(tail_body, first, count),
        out_shape=[jax.ShapeDtypeStruct((BLK, D), BF)] * count,
        in_specs=[SM] * 3 + [ANY] * 8 + [VM] * 3,
        out_specs=[VM] * count,
        scratch_shapes=[
            pltpu.VMEM((2, NG, ROWS, WID), BF),
            pltpu.VMEM((count, BLK, WID), BF),
            pltpu.VMEM((2 * BLK, SEQ), jnp.float32),
            pltpu.SemaphoreType.DMA,
        ],
        name="tail",
        cost_estimate=pl.CostEstimate(
            flops=count * (2 * BLK * D * WID + 4 * BLK * SEQ * WID),
            bytes_accessed=4 * D * WID,
            transcendentals=count * BLK * HEADS * SEQ,
        ),
    )(mod, mask, tab, *o_all, q, k, v)


def along_x(a, step):
    return lax.ppermute(a, "x", [(i, (i + step) % 4) for i in range(4)])


def along_z(a, step):
    at = [(z & 3) * 2 + (z >> 2) for z in range(8)]
    return lax.ppermute(a, ("zl", "zh"), [(at[z], at[(z + step) % 8]) for z in range(8)])


def swap(a):
    return lax.ppermute(a, "c", [(0, 1), (1, 0)])


def gather(kv, q, o, at):
    p1p, p1m = along_x(q, 1), along_x(q, -1)
    own = jnp.concatenate([kv[:1], o, kv[1:]], axis=0)
    r1p, r1m = along_z(own, 1), along_z(own, -1)
    p2 = along_x(q, 2)
    r2p, r2m = along_z(r1p[:3], 1), along_z(r1m[1:], -1)
    kb = jnp.stack(
        [
            jnp.stack([own[0], r1p[0], r1m[0], r2p[0]]),
            jnp.stack([own[3], r1p[3], r1m[3], r2m[2]]),
        ]
    )
    k1p, k1m = along_x(kb, 1), along_x(kb, -1)
    r2p, r2m = r2p[1:], r2m[:2]
    r3p, r3m = along_z(r2p, 1), along_z(r2m, -1)
    p1p, p1m, p2 = lax.optimization_barrier((p1p, p1m, p2, r3p, r3m))[:3]
    b = jnp.stack([q, p1p, p1m, p2])
    r4 = jnp.stack([along_z(r3p[0], 1), along_z(r3m[1], -1)])
    t1p, t1m = along_z(b, 1), along_z(b, -1)
    t1p, t1m, _, k1p, k1m = lax.optimization_barrier((t1p, t1m, r4, k1p, k1m))
    ob = jnp.stack([o, r1p[1:3], r1m[1:3], r2p, r2m, r3p, r3m, r4])
    o1p, o1m = along_x(ob, 1), along_x(ob, -1)
    t2p, t2m = along_z(t1p, 1), along_z(t1m, -1)
    k2p, k2m = along_x(k1p[0], 1), along_x(k1m[1], -1)
    kv_swapped = swap(jnp.concatenate([kb, k1p, k1m]))
    t2p, t2m, at = lax.optimization_barrier((t2p, t2m, at))
    tab = piece_tables(*at)
    t3p, t3m = along_z(t2p, 1), along_z(t2m, -1)
    k2p, k2m = lax.optimization_barrier((k2p, k2m, t3p, t3m))[:2]
    kv_all = [kb, k1p, k1m, k2p, k2m]
    kv_all += [kv_swapped, swap(jnp.stack([k2p, k2m]))]
    o2p, o2m = along_x(o1p[:4], 1), along_x(o1m[4:], -1)
    t4p, t4m = along_z(t3p[:2], 1), along_z(t3m[2:], -1)
    q_all = [b, t1p, t1m, t2p, t2m, t3p, t3m, t4p, t4m]
    q_all.append(swap(jnp.concatenate([b, t1p, t1m, t2p, t2m])))
    q_all += [swap(t3p), swap(t3m)]
    q_all.append(swap(jnp.concatenate([t4p, t4m])))
    o_all = [ob, o1p, o1m, o2p, o2m]
    o_all.append(swap(jnp.concatenate([ob, o1p, o1m])))
    o_all += [swap(o2p), swap(o2m)]
    return kv_all, q_all, o_all, tab


def local(tokens, modality, block_mask, q_weight, kv_weight, o_weight):
    y, zh, c = lax.axis_index("y"), lax.axis_index("zh"), lax.axis_index("c")
    at = (lax.axis_index("x"), zh * 4 + lax.axis_index("zl"), c, y)
    tables = [jnp.asarray(t) for t in rotary_tables()]
    kv = lax.dynamic_slice_in_dim(kv_weight, y * (2 * HD), 2 * HD, 2)
    kv_all, q_all, o_all, tab = gather(kv, q_weight, jnp.swapaxes(o_weight, 1, 2), at)
    small = (modality[0], block_mask[0], tab)
    q, k, v, o2a, o2b = head(*small, kv_all, q_all, o_all, tokens[0], tables)
    up = [(i, (i + 1) % NY) for i in range(NY)]
    down = [(i, (i - 1) % NY) for i in range(NY)]
    f32, half = jnp.float32, D // 2

    def add(a, b):
        return (a.astype(f32) + b.astype(f32)).astype(BF)

    far_a = lax.ppermute(o2a, "y", up)
    far_b = lax.ppermute(o2b, "y", down)
    o3, o1 = tail(3, 2, *small, o_all, q, k, v)
    p = lax.dynamic_update_slice(o1, add(o1[:, :half], far_a), (0, 0))
    m = lax.dynamic_update_slice(o3, add(o3[:, half:], far_b), (0, half))
    p = lax.ppermute(p, "y", up)
    m = lax.ppermute(m, "y", down)
    o0 = tail(0, 1, *small, o_all, q, k, v)[0]
    return (o0.astype(f32) + p.astype(f32) + m.astype(f32)).astype(BF)[None]


def solution(mesh):
    fine = Mesh(mesh.devices.reshape(4, 4, 2, 4, 2), ("x", "zl", "c", "y", "zh"))
    dp = ("x", "zl", "c")
    mp = ("y", "zh")
    in_specs = (
        P(dp, None, None),
        P(dp, None),
        P(dp, None, None),
        P(None, dp, mp),
        P(None, dp, None),
        P(None, mp, dp),
    )
    return jax.shard_map(
        local, mesh=fine, in_specs=in_specs, out_specs=P(dp, mp, None), check_vma=False
    )
```
